32 devices in a mesh: dp: 8 (over y, x, core), ctx: 4 (over z).
Axes of the slice: x: 2, y: 2, z: 4, core: 2. Of those that a mesh axis runs over, the one named last changes fastest.
Arguments:
- inputs: float32 [16, 1024, 960], P('dp', 'ctx'), may hold values from -6 to 6
- segments: int32 [16, 1024], P('dp', 'ctx'), may hold values from 0 to 9, as said below
- positions: int32 [16, 1024], P('dp', 'ctx'), may hold values from 0 to 2046, as said below
- qkv_weights: bfloat16 [2, 1536000], P(None, ('dp', 'ctx')), may hold values from -0.1875 to 0.1875
- out_weights: bfloat16 [2, 921600], P(None, ('dp', 'ctx')), may hold values from -1.5 to 1.5
- ffn_weights: bfloat16 [2, 7372800], P(None, ('dp', 'ctx')), may hold values from -0.1875 to 0.1875
- norm_gains: bfloat16 [2, 1920], P(None, ('dp', 'ctx')), may hold values from 0.099609375 to 1.8984375
- cotangent: float32 [16, 1024, 960], P('dp', 'ctx'), may hold values from -6 to 6
Outputs:
- outputs: float32 [16, 1024, 960], P('dp', 'ctx')
- input_grad: float32 [16, 1024, 960], P('dp', 'ctx')
- qkv_grad: float32 [2, 1536000], P(None, ('dp', 'ctx'))
- out_grad: float32 [2, 921600], P(None, ('dp', 'ctx'))
- ffn_grad: float32 [2, 7372800], P(None, ('dp', 'ctx'))
- gain_grad: float32 [2, 1920], P(None, ('dp', 'ctx'))
The draws below stay inside these ranges and needn't reach their ends.
Inputs may be any that keep to these rules, and one draw needn't show every extreme that they name: `segments`: within each sequence the segment numbers start at 0 and rise by one at each document's start; every document has 100 to 1024 tokens; in each aligned group of 2 sequences one sequence is a single document and another is cut into documents of 100 tokens, its last one taking the remainder. `positions`: A token's position is its document's offset, between 0 and 1023, plus its index within the document; the single-document sequence of each group has offset 1024 - 1.
All inputs are finite; a program needn't handle non-finite values.
Results may differ from the reference program's by a relative error of at most 0.029.
Values may be sent and summed in bfloat16 or wider, within the bound.
No kernel may reach another device: no remote copies, remote signals or barrier semaphores. Data moves between devices by JAX's collectives and lax.ppermute only.
A program may use at most 320 MiB of HBM per device.

```python
import math
import jax
import jax.numpy as jnp
from jax import lax

D = 960
HEADS = 15
KV_HEADS = 5
HEAD_DIM = 64
FF = 2560
LAYERS = 2
LENGTH = 1024
MIN_DOC = 100
SEQS_DEV = 2
SEQS = 16
Q_WIDTH = 960
KV_WIDTH = 320


def document_layout(key):
    base_key = jax.random.fold_in(key, 4217)
    key_len, key_pick, key_off = jax.random.split(base_key, 3)
    slot_count = LENGTH // MIN_DOC + 1
    doc_lengths = jax.random.randint(key_len, (SEQS, slot_count), MIN_DOC, LENGTH // 2 + 1)
    doc_ends = jnp.cumsum(doc_lengths, axis=1)
    doc_ends = jnp.where(doc_ends <= LENGTH - MIN_DOC, doc_ends, LENGTH + 1)
    token_index = jnp.arange(LENGTH, dtype=jnp.int32)
    passed = doc_ends[:, :, None] <= token_index[None, None, :]
    segment_ids = jnp.sum(passed.astype(jnp.int32), axis=1)
    doc_start = jnp.max(jnp.where(passed, doc_ends[:, :, None], 0), axis=1)
    chosen = jax.random.randint(key_pick, (SEQS // SEQS_DEV,), 0, SEQS_DEV)
    seq_index = jnp.arange(SEQS, dtype=jnp.int32)
    single_doc = seq_index % SEQS_DEV == jnp.repeat(chosen, SEQS_DEV)
    fine_doc = seq_index % SEQS_DEV == jnp.repeat((chosen + 1) % SEQS_DEV, SEQS_DEV)
    fine_ids = jnp.minimum(token_index // MIN_DOC, LENGTH // MIN_DOC - 1)
    segment_ids = jnp.where(fine_doc[:, None], fine_ids[None, :], segment_ids)
    doc_start = jnp.where(fine_doc[:, None], (fine_ids * MIN_DOC)[None, :], doc_start)
    segment_ids = jnp.where(single_doc[:, None], 0, segment_ids)
    doc_start = jnp.where(single_doc[:, None], 0, doc_start)
    offsets = jax.random.randint(key_off, (SEQS, slot_count + 1), 0, LENGTH)
    slot_index = jnp.arange(slot_count + 1, dtype=jnp.int32)
    offsets = jnp.where(fine_doc[:, None] & (slot_index[None, :] == 0), 0, offsets)
    offsets = jnp.where(single_doc[:, None], LENGTH - 1, offsets)
    position_ids = jnp.take_along_axis(offsets, segment_ids, axis=1) + token_index[None, :] - doc_start
    return (segment_ids.astype(jnp.int32), position_ids.astype(jnp.int32))


def draw_segments(key, part):
    return document_layout(key)[0]


def draw_positions(key, part):
    return document_layout(key)[1]


def steps_of(key, dims, shards, least, largest):
    loudness = 1.0
    for position, parts in shards:
        heights = jax.random.uniform(jax.random.fold_in(jax.random.fold_in(key, 6), position), (parts,), jnp.float32, least / len(shards), largest / len(shards))
        loudness = loudness * jnp.repeat(jnp.exp(heights), dims[position] // parts).reshape((-1,) + (1,) * (len(dims) - 1 - position))
    return loudness


def normal_values(key, extent, scale, limit, cuts=(), held_as=jnp.bfloat16):
    array = jax.random.normal(key, extent, jnp.float32) * scale
    if len(cuts) > 0:
        array = steps_of(key, extent, cuts, -0.22, 0.18) * array
    return jnp.clip(array, min=-limit, max=limit).astype(held_as)


def setup_inputs(seed: int = 0) -> dict:
    seeds = jax.random.split(jax.random.key(seed), 9)
    return {
        "inputs": normal_values(seeds[0], (SEQS, LENGTH, D), 1.0, 6.0, ((0, 8), (1, 4)), jnp.float32),
        "segments": draw_segments(jax.random.fold_in(seeds[8], 71), 0),
        "positions": draw_positions(jax.random.fold_in(seeds[8], 71), 0),
        "qkv_weights": normal_values(seeds[3], (LAYERS, D * (Q_WIDTH + 2 * KV_WIDTH)), D ** -0.5, 0.1875, ((1, 32),)),
        "out_weights": normal_values(seeds[4], (LAYERS, Q_WIDTH * D), (max(1, Q_WIDTH // 64)) ** -0.5, 1.5, ((1, 32),)),
        "ffn_weights": normal_values(seeds[5], (LAYERS, 3 * FF * D), D ** -0.5, 0.1875, ((1, 32),)),
        "norm_gains": jnp.clip(1.0 + 0.18 * jax.random.normal(seeds[6], (LAYERS, 2 * D), jnp.float32), 0.099609375, 1.8984375).astype(jnp.bfloat16),
        "cotangent": normal_values(seeds[7], (SEQS, LENGTH, D), 1.0, 6.0, ((0, 8), (1, 4)), jnp.float32),
    }


epsilon = 1e-05
rope_base = 10000.0
neg_large = -1e+30

@jax.custom_vjp
def low(v):
    return lax.optimization_barrier(v.astype(jnp.bfloat16)).astype(jnp.float32)

@jax.custom_vjp
def low_back(v):
    return v

def low_keep(v):
    return (low(v), None)

def low_pass(kept, grad):
    return (grad,)

def back_keep(v):
    return (v, None)

def back_low(kept, grad):
    return (low(grad),)
low.defvjp(low_keep, low_pass)
low_back.defvjp(back_keep, back_low)

def rms_scale(residual):
    return lax.rsqrt(lax.optimization_barrier(jnp.mean(residual * residual, -1, keepdims=True)) + epsilon)

def rotary_tables(positions):
    frequency = 1.0 / rope_base ** (jnp.arange(0, HEAD_DIM, 2, dtype=jnp.float32) / HEAD_DIM)
    angles = positions.astype(jnp.float32)[..., None] * frequency
    cosine_tab = jnp.cos(angles)
    sine_tab = jnp.sin(angles)
    return (jnp.concatenate([cosine_tab, cosine_tab], -1), jnp.concatenate([sine_tab, sine_tab], -1))

def rotate_half(tensor):
    half_dim = tensor.shape[-1] // 2
    return jnp.concatenate([-tensor[..., half_dim:], tensor[..., :half_dim]], -1)

def apply_rotary(tensor, cosine_tab, sine_tab):
    return tensor * cosine_tab + rotate_half(tensor) * sine_tab

def attend_one(query_rot, key_rot, value_low, segment_ids):
    scores = low_back(jnp.einsum('qhgd,khd->hgqk', query_rot, key_rot, precision=lax.Precision.HIGHEST) * HEAD_DIM ** (-0.5))
    token_index = jnp.arange(LENGTH, dtype=jnp.int32)
    allowed = (segment_ids[:, None] == segment_ids[None, :]) & (token_index[None, :] <= token_index[:, None])
    scores = jnp.where(allowed[None, None], scores, neg_large)
    attn_probs = low(jax.nn.softmax(scores, axis=-1))
    return jnp.einsum('hgqk,khd->qhgd', attn_probs, value_low, precision=lax.Precision.HIGHEST)

def residual_block(residual, segment_ids, positions, w_qkv, w_out, w_ffn, gain_set):
    batch_len = residual.shape[0]
    q_width = HEADS * HEAD_DIM
    kv_width = KV_HEADS * HEAD_DIM
    group_size = HEADS // KV_HEADS
    cosine_tab, sine_tab = rotary_tables(positions)
    cosine_tab = cosine_tab[:, :, None, :]
    sine_tab = sine_tab[:, :, None, :]
    normed_one = low(residual * rms_scale(residual) * gain_set[:D])
    projected = low_back(jnp.einsum('bld,de->ble', normed_one, w_qkv, precision=lax.Precision.HIGHEST))
    query_pre = projected[..., :q_width].reshape(batch_len, LENGTH, HEADS, HEAD_DIM)
    key_pre = projected[..., q_width:q_width + kv_width].reshape(batch_len, LENGTH, KV_HEADS, HEAD_DIM)
    value_low = low(projected[..., q_width + kv_width:]).reshape(batch_len, LENGTH, KV_HEADS, HEAD_DIM)
    query_rot = low(apply_rotary(query_pre, cosine_tab, sine_tab)).reshape(batch_len, LENGTH, KV_HEADS, group_size, HEAD_DIM)
    key_rot = low(apply_rotary(key_pre, cosine_tab, sine_tab))
    attend_ck = jax.checkpoint(attend_one)
    head_out = lax.map(lambda group_items: attend_ck(group_items[0], group_items[1], group_items[2], group_items[3]), (query_rot, key_rot, value_low, segment_ids))
    attended = low(low_back(head_out.reshape(batch_len, LENGTH, q_width)))
    middle = residual + low_back(jnp.einsum('ble,ed->bld', attended, w_out, precision=lax.Precision.HIGHEST))
    normed_two = low(middle * rms_scale(middle) * gain_set[D:])
    gate_val = low_back(jnp.einsum('bld,fd->blf', normed_two, w_ffn[:, 0], precision=lax.Precision.HIGHEST))
    up_val = low_back(jnp.einsum('bld,fd->blf', normed_two, w_ffn[:, 1], precision=lax.Precision.HIGHEST))
    hidden = low(jax.nn.silu(gate_val) * up_val)
    return middle + low_back(jnp.einsum('blf,fd->bld', hidden, w_ffn[:, 2], precision=lax.Precision.HIGHEST))

def reference(inputs, segments, positions, qkv_weights, out_weights, ffn_weights, norm_gains, cotangent):
    q_width = HEADS * HEAD_DIM
    kv_width = KV_HEADS * HEAD_DIM
    group_len = math.gcd(SEQS, max(1, 4096 // LENGTH))
    step_count = SEQS // group_len
    weight_set = (qkv_weights.astype(jnp.float32), out_weights.astype(jnp.float32), ffn_weights.astype(jnp.float32), norm_gains.astype(jnp.float32))

    def forward(residual, weight_all, segment_ids, position_ids):
        w_qkv_all, w_out_all, w_ffn_all, gain_all = weight_all
        for layer_idx in range(LAYERS):
            residual = residual_block(residual, segment_ids, position_ids, w_qkv_all[layer_idx].reshape(D, q_width + 2 * kv_width), w_out_all[layer_idx].reshape(q_width, D), w_ffn_all[layer_idx].reshape(FF, 3, D), gain_all[layer_idx])
        return residual

    def one_group(totals, group_items):
        residual, segment_ids, position_ids, upstream = group_items
        result, pullback = jax.vjp(lambda res_in, weight_all: forward(res_in, weight_all, segment_ids, position_ids), residual, weight_set)
        residual_grad, weight_grads = pullback(upstream)
        totals = jax.tree.map(lambda first_val, second_val: first_val + second_val, totals, weight_grads)
        return (totals, (result, residual_grad))

    def shaped(array_in):
        return array_in.reshape((step_count, group_len) + array_in.shape[1:])
    zero_grads = jax.tree.map(jnp.zeros_like, weight_set)
    totals, (result_all, grad_all) = lax.scan(one_group, zero_grads, (shaped(inputs), shaped(segments), shaped(positions), shaped(cotangent)))
    return (result_all.reshape(inputs.shape), grad_all.reshape(inputs.shape), totals[0], totals[1], totals[2], totals[3])
```

```python
import functools
import math

import jax
import jax.numpy as jnp
from jax import lax
from jax.experimental import pallas as pl
from jax.experimental.pallas import tpu as pltpu
from jax.sharding import PartitionSpec as P

D = 960
HEADS = 15
KV_HEADS = 5
GROUP = HEADS // KV_HEADS
HEAD_DIM = 64
FF = 2560
LAYERS = 2
Q_WIDTH = HEADS * HEAD_DIM
KV_WIDTH = KV_HEADS * HEAD_DIM
QKV_WIDTH = Q_WIDTH + 2 * KV_WIDTH
QK_WIDTH = Q_WIDTH + KV_WIDTH
LANES = 1024
AXES = ("dp", "ctx")

epsilon = 1e-05
rope_base = 10000.0
neg_large = -1e30
bf16 = jnp.bfloat16
f32 = jnp.float32


def dot_nn(a, b):
    return lax.dot_general(a, b, (((1,), (0,)), ((), ())), preferred_element_type=f32)


def dot_nt(a, b):
    return lax.dot_general(a, b, (((1,), (1,)), ((), ())), preferred_element_type=f32)


def dot_tn(a, b):
    return lax.dot_general(a, b, (((0,), (0,)), ((), ())), preferred_element_type=f32)


def norm_back(upstream, residual, scale_row, gain_row):
    scaled = upstream * gain_row
    return scale_row * scaled - residual * scale_row**3 * jnp.mean(
        scaled * residual, -1, keepdims=True
    )


def compiler_params():
    return pltpu.CompilerParams(vmem_limit_bytes=56 * 1024 * 1024)


def whole(shape):
    return pl.BlockSpec(shape, lambda *_: (0,) * len(shape))


def any_spec():
    return pl.BlockSpec(memory_space=pl.ANY)


def partner(value):
    half = HEAD_DIM // 2
    width = value.shape[1]
    lane = lax.broadcasted_iota(jnp.int32, value.shape, 1) % HEAD_DIM
    return jnp.where(
        lane < half, pltpu.roll(value, width - half, axis=1), pltpu.roll(value, half, axis=1)
    )


def qkv_forward_body(
    x_ref, gain_ref, qk_ref, v_ref, cos_ref, sin_ref, qk_out, v_out, normed_ref, scale_ref
):
    x = x_ref[...]
    scale = lax.rsqrt(jnp.mean(x * x, -1, keepdims=True) + epsilon)
    scale_ref[...] = scale
    normed = (x * scale * gain_ref[...]).astype(bf16)
    normed_ref[...] = normed
    block = cos_ref.shape[1]
    for j in range(QK_WIDTH // block):
        span = slice(j * block, (j + 1) * block)
        part = dot_nn(normed, qk_ref[:, span])
        qk_out[:, span] = (part * cos_ref[...] + partner(part) * sin_ref[...]).astype(bf16)
    v_out[...] = dot_nn(normed, v_ref[...]).astype(bf16)


def qkv_forward(x, gain, w_qk, w_v, cosine, sine):
    rows = x.shape[0]
    return pl.pallas_call(
        qkv_forward_body,
        out_shape=[
            jax.ShapeDtypeStruct((rows, QK_WIDTH), bf16),
            jax.ShapeDtypeStruct((rows, KV_WIDTH), bf16),
            jax.ShapeDtypeStruct((rows, D), bf16),
            jax.ShapeDtypeStruct((rows, 1), f32),
        ],
        compiler_params=compiler_params(),
        name="qkv_forward",
    )(x, gain[None], w_qk, w_v, cosine, sine)


def qkv_backward_body(
    dq_ref, dkv_ref, x_ref, normed_ref, scale_ref, gain_ref, qk_ref, v_ref, cos_ref, sin_ref,
    upstream_ref, attended_ref, low_ref, dqk_w, dov_w, dgain_ref, dx_ref, pre, low,
):
    pre[:, :Q_WIDTH] = dq_ref[...]
    pre[:, Q_WIDTH:] = dkv_ref[:, :KV_WIDTH]
    block = cos_ref.shape[1]
    normed = normed_ref[...]
    for j in range(QK_WIDTH // block):
        span = slice(j * block, (j + 1) * block)
        part = pre[:, span]
        back = (part * cos_ref[...] - partner(part) * sin_ref[...]).astype(bf16)
        low[:, span] = back
        dqk_w[:, span] = dot_tn(normed, back).astype(bf16)
    dv = dkv_ref[:, KV_WIDTH:].astype(bf16)
    dov_w[:, :Q_WIDTH] = dot_tn(attended_ref[...], low_ref[...]).astype(bf16)
    dov_w[:, Q_WIDTH:] = dot_tn(normed, dv).astype(bf16)
    normal = dot_nt(low[...], qk_ref[...]) + dot_nt(dv, v_ref[...])
    x = x_ref[...]
    scale = scale_ref[...]
    dgain_ref[...] = jnp.sum(normal * x * scale, 0, keepdims=True)
    dx_ref[...] = upstream_ref[...] + norm_back(normal, x, scale, gain_ref[...])


def qkv_backward(
    dq, dkv, x, normed, scale, gain, w_qk, w_v, cosine, sine, upstream, attended, low
):
    rows = x.shape[0]
    return pl.pallas_call(
        qkv_backward_body,
        out_shape=[
            jax.ShapeDtypeStruct((D, QK_WIDTH), bf16),
            jax.ShapeDtypeStruct((Q_WIDTH, QK_WIDTH), bf16),
            jax.ShapeDtypeStruct((1, D), f32),
            jax.ShapeDtypeStruct((rows, D), f32),
        ],
        scratch_shapes=[pltpu.VMEM((rows, QK_WIDTH), f32), pltpu.VMEM((rows, QK_WIDTH), bf16)],
        compiler_params=compiler_params(),
        name="qkv_backward",
    )(dq, dkv, x, normed, scale, gain[None], w_qk, w_v, cosine, sine, upstream, attended, low)


def ffn_forward_body(n_pieces, *refs):
    middle_ref, gain_ref = refs[:2]
    pieces = refs[2 : 2 + n_pieces]
    out_ref, normed_ref, scale_ref, gate_ref, up_ref, buffer, sems = refs[2 + n_pieces :]
    step = pl.program_id(0)

    def load(p):
        return pltpu.make_async_copy(pieces[p], buffer.at[p % 2], sems.at[p % 2])

    @pl.when(step == 0)
    def _():
        load(0).start()
        middle = middle_ref[...]
        scale = lax.rsqrt(jnp.mean(middle * middle, -1, keepdims=True) + epsilon)
        scale_ref[...] = scale
        normed_ref[...] = (middle * scale * gain_ref[...]).astype(bf16)
        out_ref[...] = middle

    for p in range(n_pieces):

        @pl.when(step == p)
        def _(p=p):
            if p + 1 < n_pieces:
                load(p + 1).start()
            load(p).wait()

    slot = step % 2
    normed = normed_ref[...]
    gate = dot_nt(normed, buffer[slot, 0, :, :D])
    up = dot_nt(normed, buffer[slot, 1, :, :D])
    gate_ref[...] = gate
    up_ref[...] = up
    hidden = (gate / (1.0 + jnp.exp(-gate)) * up).astype(bf16)
    out_ref[...] += dot_nn(hidden, buffer[slot, 2, :, :D])


def ffn_forward(middle, gain, pieces):
    rows = middle.shape[0]
    n_pieces, units = len(pieces), pieces[0].shape[1]
    tile = pl.BlockSpec((rows, units), lambda p: (0, p))
    return pl.pallas_call(
        functools.partial(ffn_forward_body, n_pieces),
        grid=(n_pieces,),
        in_specs=[whole((rows, D)), whole((1, D))] + [any_spec()] * n_pieces,
        out_specs=[whole((rows, D)), whole((rows, D)), whole((rows, 1)), tile, tile],
        out_shape=[
            jax.ShapeDtypeStruct((rows, D), f32),
            jax.ShapeDtypeStruct((rows, D), bf16),
            jax.ShapeDtypeStruct((rows, 1), f32),
            jax.ShapeDtypeStruct((rows, FF), f32),
            jax.ShapeDtypeStruct((rows, FF), f32),
        ],
        scratch_shapes=[pltpu.VMEM((2, 3, units, LANES), bf16), pltpu.SemaphoreType.DMA((2,))],
        compiler_params=compiler_params(),
        name="ffn_forward",
    )(middle, gain[None], *pieces)


def ffn_backward_body(n_pieces, *refs):
    upstream_ref, normed_ref, gate_ref, up_ref = refs[:4]
    pieces = refs[4 : 4 + n_pieces]
    grads = refs[4 + n_pieces : 4 + 2 * n_pieces]
    normal_ref, low_ref, buffer, grad_buffer, sems, out_sems = refs[4 + 2 * n_pieces :]
    step = pl.program_id(0)

    def load(p):
        return pltpu.make_async_copy(pieces[p], buffer.at[p % 2], sems.at[p % 2])

    def store(p):
        return pltpu.make_async_copy(grad_buffer.at[p % 2], grads[p], out_sems.at[p % 2])

    @pl.when(step == 0)
    def _():
        load(0).start()
        low_ref[...] = upstream_ref[...].astype(bf16)
        grad_buffer[:, :, :, D:] = jnp.zeros_like(grad_buffer[:, :, :, D:])
        normal_ref[...] = jnp.zeros_like(normal_ref)

    for p in range(n_pieces):

        @pl.when(step == p)
        def _(p=p):
            if p + 1 < n_pieces:
                load(p + 1).start()
            load(p).wait()
            if p >= 2:
                store(p - 2).wait()

    slot = step % 2
    low = low_ref[...]
    normed = normed_ref[...]
    gate = gate_ref[...]
    up = up_ref[...]
    hidden_grad = dot_nt(low, buffer[slot, 2, :, :D])
    sigmoid = 1.0 / (1.0 + jnp.exp(-gate))
    silu = gate * sigmoid
    hidden = (silu * up).astype(bf16)
    grad_buffer[slot, 2, :, :D] = dot_tn(hidden, low).astype(bf16)
    up_grad = (hidden_grad * silu).astype(bf16)
    grad_buffer[slot, 1, :, :D] = dot_tn(up_grad, normed).astype(bf16)
    gate_grad = (hidden_grad * up * sigmoid * (1.0 + gate * (1.0 - sigmoid))).astype(bf16)
    grad_buffer[slot, 0, :, :D] = dot_tn(gate_grad, normed).astype(bf16)
    for p in range(n_pieces):

        @pl.when(step == p)
        def _(p=p):
            store(p).start()

    normal_ref[...] += dot_nn(gate_grad, buffer[slot, 0, :, :D]) + dot_nn(
        up_grad, buffer[slot, 1, :, :D]
    )

    @pl.when(step == n_pieces - 1)
    def _():
        for p in range(max(0, n_pieces - 2), n_pieces):
            store(p).wait()


def ffn_backward(upstream, normed, gate, up, pieces):
    rows = upstream.shape[0]
    n_pieces, units = len(pieces), pieces[0].shape[1]
    tile = pl.BlockSpec((rows, units), lambda p: (0, p))
    result = pl.pallas_call(
        functools.partial(ffn_backward_body, n_pieces),
        grid=(n_pieces,),
        in_specs=[whole((rows, D)), whole((rows, D)), tile, tile] + [any_spec()] * n_pieces,
        out_specs=[any_spec()] * n_pieces + [whole((rows, D))],
        out_shape=[jax.ShapeDtypeStruct((3, units, LANES), bf16)] * n_pieces
        + [jax.ShapeDtypeStruct((rows, D), f32)],
        scratch_shapes=[
            pltpu.VMEM((rows, D), bf16),
            pltpu.VMEM((2, 3, units, LANES), bf16),
            pltpu.VMEM((2, 3, units, LANES), bf16),
            pltpu.SemaphoreType.DMA((2,)),
            pltpu.SemaphoreType.DMA((2,)),
        ],
        compiler_params=compiler_params(),
        name="ffn_backward",
    )(upstream, normed, gate, up, *pieces)
    return result[:n_pieces], result[n_pieces]


def mask_bias(key_info, query_info, local_len, half_keys):
    parts = []
    for side in range(2):
        count = half_keys * (side + 1)
        token, segment = key_info[:count, 0:1], key_info[:count, 1:2]
        span = slice(side * local_len, (side + 1) * local_len)
        q_token, q_segment = query_info[0:1, span], query_info[1:2, span]
        parts.append(jnp.where((segment == q_segment) & (token <= q_token), 0.0, neg_large))
    return parts


def attention_forward_body(
    q_ref, kv_ref, key_info, query_info, o_ref, lse_ref, qs, ks, vts, os, bias_low, bias_high
):
    rows = q_ref.shape[0]
    local_len, half_keys = rows // 2, kv_ref.shape[0] // 2
    bias_low[...], bias_high[...] = mask_bias(
        key_info[...], query_info[...], local_len, half_keys
    )
    for h in range(HEADS):
        qs[h] = q_ref[:, h * HEAD_DIM : (h + 1) * HEAD_DIM]
    for h in range(KV_HEADS):
        ks[h] = kv_ref[:, h * HEAD_DIM : (h + 1) * HEAD_DIM]
        value = kv_ref[:, KV_WIDTH + h * HEAD_DIM : KV_WIDTH + (h + 1) * HEAD_DIM]
        vts[h] = value.astype(f32).T.astype(bf16)

    def group(g, carry):
        for i in range(GROUP):
            h = g * GROUP + i
            for side, bias in enumerate((bias_low, bias_high)):
                count = half_keys * (side + 1)
                span = slice(side * local_len, (side + 1) * local_len)
                scores = dot_nt(ks[g, :count], qs[h, span]) * HEAD_DIM**-0.5 + bias[...]
                top = jnp.max(scores, 0, keepdims=True)
                probs = jnp.exp(scores - top)
                total = jnp.sum(probs, 0, keepdims=True)
                out = dot_nn(vts[g, :, :count], probs.astype(bf16)) / total
                os[h, span] = out.T.astype(bf16)
                lse_ref[h, :, span] = top + jnp.log(total)
        return carry

    lax.fori_loop(0, KV_HEADS, group, 0)
    for h in range(HEADS):
        o_ref[:, h * HEAD_DIM : (h + 1) * HEAD_DIM] = os[h]


def attention_forward(query, kv, key_info, query_info):
    rows, keys = query.shape[0], kv.shape[0]
    return pl.pallas_call(
        attention_forward_body,
        out_shape=[
            jax.ShapeDtypeStruct((rows, Q_WIDTH), bf16),
            jax.ShapeDtypeStruct((HEADS, 1, rows), f32),
        ],
        scratch_shapes=[
            pltpu.VMEM((HEADS, rows, HEAD_DIM), bf16),
            pltpu.VMEM((KV_HEADS, keys, HEAD_DIM), bf16),
            pltpu.VMEM((KV_HEADS, HEAD_DIM, keys), bf16),
            pltpu.VMEM((HEADS, rows, HEAD_DIM), bf16),
            pltpu.VMEM((keys // 2, rows // 2), f32),
            pltpu.VMEM((keys, rows // 2), f32),
        ],
        compiler_params=compiler_params(),
        name="attention_forward",
    )(query, kv, key_info, query_info)


def attention_backward_body(
    q_ref, kv_ref, og_ref, lse_ref, key_info, query_info, dq_ref, dkv_ref,
    qs, gs, ks, kts, vs, dqs, dks, dvs, bias_low, bias_high,
):
    rows = q_ref.shape[0]
    local_len, half_keys = rows // 2, kv_ref.shape[0] // 2
    bias_low[...], bias_high[...] = mask_bias(
        key_info[...], query_info[...], local_len, half_keys
    )
    for h in range(HEADS):
        qs[h] = q_ref[:, h * HEAD_DIM : (h + 1) * HEAD_DIM]
        gs[h] = og_ref[:, h * HEAD_DIM : (h + 1) * HEAD_DIM]
    for h in range(KV_HEADS):
        key = kv_ref[:, h * HEAD_DIM : (h + 1) * HEAD_DIM]
        ks[h] = key
        kts[h] = key.astype(f32).T.astype(bf16)
        vs[h] = kv_ref[:, KV_WIDTH + h * HEAD_DIM : KV_WIDTH + (h + 1) * HEAD_DIM]

    def group(g, carry):
        for i in range(GROUP):
            h = g * GROUP + i
            for side, bias in enumerate((bias_low, bias_high)):
                count = half_keys * (side + 1)
                span = slice(side * local_len, (side + 1) * local_len)
                query, grad = qs[h, span], gs[h, span]
                scores = dot_nt(ks[g, :count], query) * HEAD_DIM**-0.5 + bias[...]
                probs = jnp.exp(scores - lse_ref[h, :, span])
                prob_grad = dot_nt(vs[g, :count], grad)
                delta = jnp.sum(probs * prob_grad, 0, keepdims=True)
                score_grad = (probs * (prob_grad - delta)).astype(bf16)
                value_part = dot_nn(probs.astype(bf16), grad)
                key_part = dot_nn(score_grad, query)
                dqs[h, span] = dot_nn(kts[g, :, :count], score_grad).T * HEAD_DIM**-0.5
                if i == 0 and side == 0:
                    dks[g, :count] = key_part
                    dvs[g, :count] = value_part
                    dks[g, count:] = jnp.zeros_like(key_part)
                    dvs[g, count:] = jnp.zeros_like(value_part)
                else:
                    dks[g, :count] += key_part
                    dvs[g, :count] += value_part
        return carry

    lax.fori_loop(0, KV_HEADS, group, 0)
    for h in range(HEADS):
        dq_ref[:, h * HEAD_DIM : (h + 1) * HEAD_DIM] = dqs[h]
    for h in range(KV_HEADS):
        dkv_ref[:, h * HEAD_DIM : (h + 1) * HEAD_DIM] = dks[h] * HEAD_DIM**-0.5
        dkv_ref[:, KV_WIDTH + h * HEAD_DIM : KV_WIDTH + (h + 1) * HEAD_DIM] = dvs[h]


def attention_backward(query, kv, out_grad, lse, key_info, query_info):
    rows, keys = query.shape[0], kv.shape[0]
    return pl.pallas_call(
        attention_backward_body,
        out_shape=[
            jax.ShapeDtypeStruct((rows, Q_WIDTH), f32),
            jax.ShapeDtypeStruct((keys, 2 * KV_WIDTH), f32),
        ],
        scratch_shapes=[
            pltpu.VMEM((HEADS, rows, HEAD_DIM), bf16),
            pltpu.VMEM((HEADS, rows, HEAD_DIM), bf16),
            pltpu.VMEM((KV_HEADS, keys, HEAD_DIM), bf16),
            pltpu.VMEM((KV_HEADS, HEAD_DIM, keys), bf16),
            pltpu.VMEM((KV_HEADS, keys, HEAD_DIM), bf16),
            pltpu.VMEM((HEADS, rows, HEAD_DIM), f32),
            pltpu.VMEM((KV_HEADS, keys, HEAD_DIM), f32),
            pltpu.VMEM((KV_HEADS, keys, HEAD_DIM), f32),
            pltpu.VMEM((keys // 2, rows // 2), f32),
            pltpu.VMEM((keys, rows // 2), f32),
        ],
        compiler_params=compiler_params(),
        name="attention_backward",
    )(query, kv, out_grad, lse, key_info, query_info)


def exchange(value, dp_xor=0, ctx_xor=0):
    n_dp, n_ctx = lax.axis_size("dp"), lax.axis_size("ctx")
    pairs = [
        (d * n_ctx + c, (d ^ dp_xor) * n_ctx + (c ^ ctx_xor))
        for d in range(n_dp)
        for c in range(n_ctx)
    ]
    return lax.ppermute(value, AXES, pairs)


def dp_bits(color):
    n_dp = lax.axis_size("dp")
    high = [1 << i for i in range(1, n_dp.bit_length() - 1)]
    return (high[::-1] if color else high) + [1]


def bit_set(axis_name, bit):
    return (lax.axis_index(axis_name) & bit) != 0


class Job:
    def __init__(self, chain):
        self.chain = chain
        self.result = None
        self.pending = next(chain)

    def step(self, arrived):
        try:
            self.pending = self.chain.send(arrived)
        except StopIteration as stop:
            self.pending, self.result = None, stop.value


def fence(values, *jobs):
    live = [job for job in jobs if job.pending is not None]
    values, arrived = lax.optimization_barrier((values, [job.pending for job in live]))
    for job, arrays in zip(live, arrived):
        job.step(arrays)
    return values


def finish(values, *jobs):
    while any(job.pending is not None for job in jobs):
        values = fence(values, *jobs)
    return values


def ctx_ordered(parts):
    n = len(parts)
    for i in range(n.bit_length() - 1):
        flag = bit_set("ctx", 1 << i)
        parts = [jnp.where(flag, parts[k ^ (1 << i)], parts[k]) for k in range(n)]
    return parts


def ctx_stage(value):
    return [exchange(value, ctx_xor=k) for k in range(1, lax.axis_size("ctx"))]


def gather_ffn_job(flat):
    units = flat.shape[0] // (3 * D)
    half = units // 2
    block = jnp.pad(flat.reshape(units, 3, D), ((0, 0), (0, 0), (0, LANES - D))).transpose(1, 0, 2)
    (block,) = yield [block]
    parts = [block] + (yield ctx_stage(block))
    sides = [jnp.concatenate([p[:, :half] for p in parts], 1)]
    sides += [jnp.concatenate([p[:, half:] for p in parts], 1)]
    orders = [dp_bits(color) for color in range(2)]
    for i in range(len(orders[0])):
        arrived = yield [exchange(s, dp_xor=order[i]) for s, order in zip(sides, orders)]
        if i + 1 < len(orders[0]):
            sides = [jnp.concatenate([s, a], 1) for s, a in zip(sides, arrived)]
    return [sides[0], arrived[0], sides[1], arrived[1]]


def scatter_ffn_job(pieces, shard_len):
    orders = [dp_bits(color)[::-1] for color in range(2)]
    keeps, sends = [pieces[0], pieces[2]], [pieces[1], pieces[3]]
    for i in range(len(orders[0])):
        arrived = yield [exchange(s, dp_xor=order[i]) for s, order in zip(sends, orders)]
        totals = [(k.astype(f32) + a.astype(f32)).astype(bf16) for k, a in zip(keeps, arrived)]
        if i + 1 < len(orders[0]):
            half = totals[0].shape[1] // 2
            keeps, sends = [t[:, :half] for t in totals], [t[:, half:] for t in totals]
    n_ctx = lax.axis_size("ctx")
    half = totals[0].shape[1] // n_ctx
    parts = [
        jnp.concatenate([t[:, k * half : (k + 1) * half] for t in totals], 1)
        for k in range(n_ctx)
    ]
    arrived = yield [exchange(parts[k], ctx_xor=k) for k in range(1, n_ctx)]
    shard = parts[0].astype(f32)
    for part in arrived:
        shard = shard + part.astype(f32)
    return shard[:, :, :D].transpose(1, 0, 2).reshape(shard_len)


def add_row(block, row):
    pad = jnp.zeros((1, block.shape[1] - row.shape[0]), block.dtype)
    return jnp.concatenate([block, jnp.concatenate([row[None], pad], 1)], 0)


def by_rows(shard_len):
    return shard_len % QKV_WIDTH == 0


def gather_attention_job(qkv_flat, out_flat, gain_flat):
    n_dp, n_ctx = lax.axis_size("dp"), lax.axis_size("ctx")
    n, n_bits = n_dp * n_ctx, n_dp.bit_length() - 1
    gain_len = gain_flat.shape[0]
    if by_rows(qkv_flat.shape[0]):
        qkv, out = qkv_flat.reshape(-1, QKV_WIDTH), out_flat.reshape(-1, D)
        blocks = [add_row(qkv[:, :QK_WIDTH], gain_flat)]
        blocks += [add_row(jnp.concatenate([out, qkv[:, QK_WIDTH:]], 1), gain_flat)]
        (both,) = yield [jnp.concatenate(blocks, 1)]
        parts = ctx_ordered([both] + (yield ctx_stage(both)))
        sides = [[p[:, :QK_WIDTH] for p in parts], [p[:, QK_WIDTH:] for p in parts]]
    else:
        qkv_cols = math.gcd(qkv_flat.shape[0], QKV_WIDTH)
        out_cols = math.gcd(out_flat.shape[0], D)
        blocks = [add_row(qkv_flat.reshape(-1, qkv_cols), gain_flat)]
        blocks += [out_flat.reshape(-1, out_cols)]
        blocks = yield blocks
        arrived = yield ctx_stage(blocks[0]) + ctx_stage(blocks[1])
        sides = [
            ctx_ordered([blocks[0]] + arrived[: n_ctx - 1]),
            ctx_ordered([blocks[1]] + arrived[n_ctx - 1 :]),
        ]
    sides = [jnp.stack(p, 0).reshape((1,) * n_bits + (n_ctx,) + p[0].shape) for p in sides]
    orders = [dp_bits(color) for color in range(2)]
    for i in range(n_bits):
        arrived = yield [exchange(s, dp_xor=order[i]) for s, order in zip(sides, orders)]
        joined = []
        for mine, other, order in zip(sides, arrived, orders):
            flag = bit_set("dp", order[i])
            pair = [jnp.where(flag, other, mine), jnp.where(flag, mine, other)]
            joined.append(jnp.concatenate(pair, n_bits - order[i].bit_length()))
        sides = joined
    first, second = (s.reshape((n,) + s.shape[-2:]) for s in sides)
    gains = first[:, -1, :gain_len].reshape(n * gain_len).astype(f32)
    if by_rows(qkv_flat.shape[0]):
        w_qk = first[:, :-1].reshape(D, QK_WIDTH)
        second = second[:, :-1].reshape(D, QK_WIDTH)
        w_out, w_v = second[:, :D], second[:, D:]
    else:
        w_qkv = first[:, :-1].reshape(D, QKV_WIDTH)
        w_qk, w_v = w_qkv[:, :QK_WIDTH], w_qkv[:, QK_WIDTH:]
        w_out = second.reshape(Q_WIDTH, D)
    return w_qk, w_v, w_out, gains[:D], gains[D:]


def scatter_attention_job(dw_qk, dw_ov, gain_grad, qkv_len, out_len):
    n_dp, n_ctx = lax.axis_size("dp"), lax.axis_size("ctx")
    n, n_bits = n_dp * n_ctx, n_dp.bit_length() - 1
    gain_len = gain_grad.shape[0] // n
    gain_row = gain_grad.astype(bf16).reshape(n, 1, gain_len)

    def with_gain(blocks):
        return jnp.concatenate(
            [blocks, jnp.pad(gain_row, ((0, 0), (0, 0), (0, blocks.shape[2] - gain_len)))], 1
        )

    if by_rows(qkv_len):
        sides = [with_gain(dw_qk.reshape(n, -1, QK_WIDTH)), dw_ov.reshape(n, -1, QK_WIDTH)]
    else:
        dw_qkv = jnp.concatenate([dw_qk, dw_ov[:, Q_WIDTH:]], 1)
        sides = [with_gain(dw_qkv.reshape(n, -1, math.gcd(qkv_len, QKV_WIDTH)))]
        sides += [dw_ov[:, :Q_WIDTH].reshape(n, -1, math.gcd(out_len, D))]
    sides = [s.reshape((2,) * n_bits + (n_ctx,) + s.shape[1:]) for s in sides]
    orders = [dp_bits(color)[::-1] for color in range(2)]
    for i in range(n_bits):
        keeps, sends = [], []
        for side, order in zip(sides, orders):
            low, high = jnp.split(side, 2, n_bits - order[i].bit_length())
            flag = bit_set("dp", order[i])
            keeps.append(jnp.where(flag, high, low))
            sends.append(jnp.where(flag, low, high))
        arrived = yield [exchange(s, dp_xor=order[i]) for s, order in zip(sends, orders)]
        sides = [(k.astype(f32) + a.astype(f32)).astype(bf16) for k, a in zip(keeps, arrived)]
    parts = [ctx_ordered(list(s.reshape((n_ctx,) + s.shape[-2:]))) for s in sides]
    arrived = yield [exchange(p[k], ctx_xor=k) for p in parts for k in range(1, n_ctx)]
    totals = []
    for i in range(2):
        total = parts[i][0].astype(f32)
        for part in arrived[i * (n_ctx - 1) : (i + 1) * (n_ctx - 1)]:
            total = total + part.astype(f32)
        totals.append(total)
    first, second = totals
    gain_part = first[-1, :gain_len]
    if by_rows(qkv_len):
        qkv_part = jnp.concatenate([first[:-1], second[:, D:]], 1)
        out_part = second[:, :D]
    else:
        qkv_part, out_part = first[:-1], second
    return qkv_part.reshape(qkv_len), out_part.reshape(out_len), gain_part


def low_side():
    return lax.axis_index("ctx") < lax.axis_size("ctx") // 2


def pair_tokens_job(value, wire):
    low = low_side()
    keep = jnp.where(low, value[0], value[1])
    send = jnp.where(low, value[1], value[0]).astype(wire)
    (send,) = yield [send]
    (other,) = yield [exchange(send, ctx_xor=lax.axis_size("ctx") - 1)]
    other = other.astype(value.dtype)
    return jnp.stack([jnp.where(low, keep, other), jnp.where(low, other, keep)], 0)


def gather_group(value):
    n = lax.axis_size("ctx") // 2
    parts = [value] + [exchange(value, ctx_xor=k) for k in range(1, n)]
    return jnp.concatenate([p[0] for p in parts] + [p[1] for p in parts], 0)


def scatter_group(value):
    n = lax.axis_size("ctx") // 2
    parts = value.reshape((2, n, value.shape[0] // (2 * n)) + value.shape[1:])
    result = parts[:, 0].astype(f32)
    for k in range(1, n):
        result = result + exchange(parts[:, k].astype(bf16), ctx_xor=k).astype(f32)
    return result


def per_device(
    inputs, segments, positions, qkv_weights, out_weights, ffn_weights, norm_gains, cotangent
):
    seq_count, local_len, _ = inputs.shape
    assert seq_count == 2
    n_ctx = lax.axis_size("ctx")
    rows = 2 * local_len
    qkv_len, out_len, ffn_len = qkv_weights.shape[1], out_weights.shape[1], ffn_weights.shape[1]

    tokens = Job(pair_tokens_job(inputs, bf16))
    upstream = Job(pair_tokens_job(cotangent, bf16))
    info = Job(pair_tokens_job(jnp.stack([segments, positions], 2), jnp.int32))
    attn = [
        Job(gather_attention_job(qkv_weights[i], out_weights[i], norm_gains[i]))
        for i in range(LAYERS)
    ]
    ffn = [Job(gather_ffn_job(ffn_weights[i])) for i in range(LAYERS)]

    fence((), attn[0], info)
    fence((), attn[0], info, tokens)
    fence((), attn[0], ffn[0])
    fence((), attn[0], tokens)
    finish((), attn[0], info, tokens)
    info = info.result

    index = lax.axis_index("ctx")
    early = jnp.minimum(index, n_ctx - 1 - index)
    within = jnp.arange(local_len, dtype=jnp.int32)
    token_own = jnp.stack([early * local_len + within, (n_ctx - 1 - early) * local_len + within])
    segment_own, position_own = info[..., 0], info[..., 1].reshape(rows)
    info_own = jnp.stack([token_own, segment_own], 2)
    key_info = gather_group(info_own)
    query_info = info_own.reshape(rows, 2).T

    frequency = 1.0 / rope_base ** (jnp.arange(0, HEAD_DIM, 2, dtype=f32) / HEAD_DIM)
    angles = position_own[:, None].astype(f32) * frequency
    cosine, sine = jnp.cos(angles), jnp.sin(angles)
    cosine = jnp.tile(cosine, (1, 8))
    sine = jnp.tile(jnp.concatenate([-sine, sine], 1), (1, 4))

    residual = tokens.result.reshape(rows, D)
    saved = []
    for layer in range(LAYERS):
        w_qk, w_v, w_out, gain_one, gain_two = attn[layer].result
        qk, value, normed_one, scale_one = qkv_forward(residual, gain_one, w_qk, w_v, cosine, sine)
        qk, value = fence((qk, value), ffn[layer])
        kv_own = jnp.concatenate([qk[:, Q_WIDTH:], value], 1)
        kv_all = gather_group(kv_own.reshape(2, local_len, 2 * KV_WIDTH))
        if layer == 0:
            qk, kv_all = fence((qk, kv_all), ffn[0], attn[1])
        attended, lse = attention_forward(qk, kv_all, key_info, query_info)
        middle = residual + dot_nn(attended, w_out)
        if layer == 0:
            middle = fence(middle, ffn[1], attn[1])
            middle = fence(middle, ffn[0])
            middle = fence(middle, ffn[0], attn[1])
        else:
            middle = fence(middle, ffn[1], upstream)
        middle = finish(middle, ffn[layer])
        following, normed_two, scale_two, gate, up = ffn_forward(
            middle, gain_two, ffn[layer].result
        )
        saved.append(
            (residual, scale_one, normed_one, qk, kv_all, lse, attended)
            + (middle, scale_two, normed_two, gate, up)
        )
        residual = following
        if layer == 0:
            residual = fence(residual, attn[1], ffn[1], upstream)
            residual = finish(residual, attn[1])
    residual = finish(residual, upstream)
    back = Job(pair_tokens_job(residual.reshape(2, local_len, D), bf16))
    gradient = upstream.result.reshape(rows, D)

    attn_jobs, ffn_jobs = [None] * LAYERS, [None] * LAYERS
    for layer in reversed(range(LAYERS)):
        w_qk, w_v, w_out, gain_one, gain_two = attn[layer].result
        residual, scale_one, normed_one, qk, kv_all, lse, attended = saved[layer][:7]
        middle, scale_two, normed_two, gate, up = saved[layer][7:]
        terms, normal_two = ffn_backward(gradient, normed_two, gate, up, ffn[layer].result)
        if layer:
            terms, normal_two = fence((terms, normal_two), back)
        else:
            terms, normal_two = fence((terms, normal_two), ffn_jobs[1], attn_jobs[1])
        ffn_jobs[layer] = Job(scatter_ffn_job(terms, ffn_len))
        gain_two_grad = jnp.sum(normal_two * middle * scale_two, 0)
        gradient = gradient + norm_back(normal_two, middle, scale_two, gain_two)
        attn_low = gradient.astype(bf16)
        attended_grad = dot_nt(attn_low, w_out).astype(bf16)
        attended_grad = fence(attended_grad, ffn_jobs[layer], back if layer else attn_jobs[1])
        query_grad, kv_grad = attention_backward(
            qk, kv_all, attended_grad, lse, key_info, query_info
        )
        if layer == 0:
            query_grad, kv_grad = fence((query_grad, kv_grad), ffn_jobs[1], attn_jobs[1])
        kv_grad = scatter_group(kv_grad).reshape(rows, 2 * KV_WIDTH)
        dw_qk, dw_ov, gain_one_grad, gradient = qkv_backward(
            query_grad, kv_grad, residual, normed_one, scale_one, gain_one, w_qk, w_v,
            cosine, sine, gradient, attended, attn_low,
        )
        dw_qk, dw_ov, gradient = fence((dw_qk, dw_ov, gradient), ffn_jobs[layer])
        attn_jobs[layer] = Job(
            scatter_attention_job(
                dw_qk, dw_ov, jnp.concatenate([gain_one_grad[0], gain_two_grad]), qkv_len, out_len
            )
        )
    last = Job(pair_tokens_job(gradient.reshape(2, local_len, D), bf16))
    fence((), last)
    fence((), ffn_jobs[0], attn_jobs[0], attn_jobs[1], last)
    fence((), attn_jobs[0])
    fence((), attn_jobs[0], ffn_jobs[0])
    finish((), back, last, *ffn_jobs, *attn_jobs)
    return (
        back.result,
        last.result,
        jnp.stack([job.result[0] for job in attn_jobs]),
        jnp.stack([job.result[1] for job in attn_jobs]),
        jnp.stack([job.result for job in ffn_jobs]),
        jnp.stack([job.result[2] for job in attn_jobs]),
    )


def solution(mesh):
    tokens = P("dp", "ctx", None)
    shards = P(None, ("dp", "ctx"))
    return jax.shard_map(
        per_device,
        mesh=mesh,
        in_specs=(tokens, P("dp", "ctx"), P("dp", "ctx"), shards, shards, shards, shards, tokens),
        out_specs=(tokens, tokens, shards, shards, shards, shards),
        check_vma=False,
    )
```

```python
import functools
import math

import jax
import jax.numpy as jnp
from jax import lax
from jax.experimental import pallas as pl
from jax.experimental.pallas import tpu as pltpu
from jax.sharding import PartitionSpec as P

D = 960
HEADS = 15
KV_HEADS = 5
GROUP = HEADS // KV_HEADS
HEAD_DIM = 64
FF = 2560
LAYERS = 2
Q_WIDTH = HEADS * HEAD_DIM
KV_WIDTH = KV_HEADS * HEAD_DIM
QKV_WIDTH = Q_WIDTH + 2 * KV_WIDTH
QK_WIDTH = Q_WIDTH + KV_WIDTH
LANES = 1024
AXES = ("dp", "ctx")

epsilon = 1e-05
rope_base = 10000.0
neg_large = -1e30
bf16 = jnp.bfloat16
f32 = jnp.float32


def dot_nn(a, b):
    return lax.dot_general(a, b, (((1,), (0,)), ((), ())), preferred_element_type=f32)


def dot_nt(a, b):
    return lax.dot_general(a, b, (((1,), (1,)), ((), ())), preferred_element_type=f32)


def dot_tn(a, b):
    return lax.dot_general(a, b, (((0,), (0,)), ((), ())), preferred_element_type=f32)


def norm_back(upstream, residual, scale_row, gain_row):
    scaled = upstream * gain_row
    return scale_row * scaled - residual * scale_row**3 * jnp.mean(
        scaled * residual, -1, keepdims=True
    )


def compiler_params():
    return pltpu.CompilerParams(vmem_limit_bytes=56 * 1024 * 1024)


def whole(shape):
    return pl.BlockSpec(shape, lambda *_: (0,) * len(shape))


def any_spec():
    return pl.BlockSpec(memory_space=pl.ANY)


def partner(value):
    half = HEAD_DIM // 2
    width = value.shape[1]
    lane = lax.broadcasted_iota(jnp.int32, value.shape, 1) % HEAD_DIM
    return jnp.where(
        lane < half, pltpu.roll(value, width - half, axis=1), pltpu.roll(value, half, axis=1)
    )


def qkv_forward_body(
    x_ref, gain_ref, qk_ref, v_ref, cos_ref, sin_ref, qk_out, v_out, normed_ref, scale_ref
):
    x = x_ref[...]
    scale = lax.rsqrt(jnp.mean(x * x, -1, keepdims=True) + epsilon)
    scale_ref[...] = scale
    normed = (x * scale * gain_ref[...]).astype(bf16)
    normed_ref[...] = normed
    block = cos_ref.shape[1]
    for j in range(QK_WIDTH // block):
        span = slice(j * block, (j + 1) * block)
        part = dot_nn(normed, qk_ref[:, span])
        qk_out[:, span] = (part * cos_ref[...] + partner(part) * sin_ref[...]).astype(bf16)
    v_out[...] = dot_nn(normed, v_ref[...]).astype(bf16)


def qkv_forward(x, gain, w_qk, w_v, cosine, sine):
    rows = x.shape[0]
    return pl.pallas_call(
        qkv_forward_body,
        out_shape=[
            jax.ShapeDtypeStruct((rows, QK_WIDTH), bf16),
            jax.ShapeDtypeStruct((rows, KV_WIDTH), bf16),
            jax.ShapeDtypeStruct((rows, D), bf16),
            jax.ShapeDtypeStruct((rows, 1), f32),
        ],
        compiler_params=compiler_params(),
        name="qkv_forward",
    )(x, gain[None], w_qk, w_v, cosine, sine)


def qkv_backward_body(
    dq_ref, dkv_ref, x_ref, normed_ref, scale_ref, gain_ref, qk_ref, v_ref, cos_ref, sin_ref,
    upstream_ref, attended_ref, low_ref, dqk_w, dov_w, dgain_ref, dx_ref, pre, low,
):
    pre[:, :Q_WIDTH] = dq_ref[...]
    pre[:, Q_WIDTH:] = dkv_ref[:, :KV_WIDTH]
    block = cos_ref.shape[1]
    normed = normed_ref[...]
    for j in range(QK_WIDTH // block):
        span = slice(j * block, (j + 1) * block)
        part = pre[:, span]
        back = (part * cos_ref[...] - partner(part) * sin_ref[...]).astype(bf16)
        low[:, span] = back
        dqk_w[:, span] = dot_tn(normed, back).astype(bf16)
    dv = dkv_ref[:, KV_WIDTH:].astype(bf16)
    dov_w[:, :Q_WIDTH] = dot_tn(attended_ref[...], low_ref[...]).astype(bf16)
    dov_w[:, Q_WIDTH:] = dot_tn(normed, dv).astype(bf16)
    normal = dot_nt(low[...], qk_ref[...]) + dot_nt(dv, v_ref[...])
    x = x_ref[...]
    scale = scale_ref[...]
    dgain_ref[...] = jnp.sum(normal * x * scale, 0, keepdims=True)
    dx_ref[...] = upstream_ref[...] + norm_back(normal, x, scale, gain_ref[...])


def qkv_backward(
    dq, dkv, x, normed, scale, gain, w_qk, w_v, cosine, sine, upstream, attended, low
):
    rows = x.shape[0]
    return pl.pallas_call(
        qkv_backward_body,
        out_shape=[
            jax.ShapeDtypeStruct((D, QK_WIDTH), bf16),
            jax.ShapeDtypeStruct((Q_WIDTH, QK_WIDTH), bf16),
            jax.ShapeDtypeStruct((1, D), f32),
            jax.ShapeDtypeStruct((rows, D), f32),
        ],
        scratch_shapes=[pltpu.VMEM((rows, QK_WIDTH), f32), pltpu.VMEM((rows, QK_WIDTH), bf16)],
        compiler_params=compiler_params(),
        name="qkv_backward",
    )(dq, dkv, x, normed, scale, gain[None], w_qk, w_v, cosine, sine, upstream, attended, low)


def ffn_forward_body(n_pieces, *refs):
    middle_ref, gain_ref = refs[:2]
    pieces = refs[2 : 2 + n_pieces]
    out_ref, normed_ref, scale_ref, gate_ref, up_ref, buffer, sems = refs[2 + n_pieces :]
    step = pl.program_id(0)

    def load(p):
        return pltpu.make_async_copy(pieces[p], buffer.at[p % 2], sems.at[p % 2])

    @pl.when(step == 0)
    def _():
        load(0).start()
        middle = middle_ref[...]
        scale = lax.rsqrt(jnp.mean(middle * middle, -1, keepdims=True) + epsilon)
        scale_ref[...] = scale
        normed_ref[...] = (middle * scale * gain_ref[...]).astype(bf16)
        out_ref[...] = middle

    for p in range(n_pieces):

        @pl.when(step == p)
        def _(p=p):
            if p + 1 < n_pieces:
                load(p + 1).start()
            load(p).wait()

    slot = step % 2
    normed = normed_ref[...]
    gate = dot_nt(normed, buffer[slot, 0, :, :D])
    up = dot_nt(normed, buffer[slot, 1, :, :D])
    gate_ref[...] = gate
    up_ref[...] = up
    hidden = (gate / (1.0 + jnp.exp(-gate)) * up).astype(bf16)
    out_ref[...] += dot_nn(hidden, buffer[slot, 2, :, :D])


def ffn_forward(middle, gain, pieces):
    rows = middle.shape[0]
    n_pieces, units = len(pieces), pieces[0].shape[1]
    tile = pl.BlockSpec((rows, units), lambda p: (0, p))
    return pl.pallas_call(
        functools.partial(ffn_forward_body, n_pieces),
        grid=(n_pieces,),
        in_specs=[whole((rows, D)), whole((1, D))] + [any_spec()] * n_pieces,
        out_specs=[whole((rows, D)), whole((rows, D)), whole((rows, 1)), tile, tile],
        out_shape=[
            jax.ShapeDtypeStruct((rows, D), f32),
            jax.ShapeDtypeStruct((rows, D), bf16),
            jax.ShapeDtypeStruct((rows, 1), f32),
            jax.ShapeDtypeStruct((rows, FF), f32),
            jax.ShapeDtypeStruct((rows, FF), f32),
        ],
        scratch_shapes=[pltpu.VMEM((2, 3, units, LANES), bf16), pltpu.SemaphoreType.DMA((2,))],
        compiler_params=compiler_params(),
        name="ffn_forward",
    )(middle, gain[None], *pieces)


def ffn_backward_body(n_pieces, *refs):
    upstream_ref, normed_ref, gate_ref, up_ref = refs[:4]
    pieces = refs[4 : 4 + n_pieces]
    grads = refs[4 + n_pieces : 4 + 2 * n_pieces]
    normal_ref, low_ref, buffer, grad_buffer, sems, out_sems = refs[4 + 2 * n_pieces :]
    step = pl.program_id(0)

    def load(p):
        return pltpu.make_async_copy(pieces[p], buffer.at[p % 2], sems.at[p % 2])

    def store(p):
        return pltpu.make_async_copy(grad_buffer.at[p % 2], grads[p], out_sems.at[p % 2])

    @pl.when(step == 0)
    def _():
        load(0).start()
        low_ref[...] = upstream_ref[...].astype(bf16)
        grad_buffer[:, :, :, D:] = jnp.zeros_like(grad_buffer[:, :, :, D:])
        normal_ref[...] = jnp.zeros_like(normal_ref)

    for p in range(n_pieces):

        @pl.when(step == p)
        def _(p=p):
            if p + 1 < n_pieces:
                load(p + 1).start()
            load(p).wait()
            if p >= 2:
                store(p - 2).wait()

    slot = step % 2
    low = low_ref[...]
    normed = normed_ref[...]
    gate = gate_ref[...]
    up = up_ref[...]
    hidden_grad = dot_nt(low, buffer[slot, 2, :, :D])
    sigmoid = 1.0 / (1.0 + jnp.exp(-gate))
    silu = gate * sigmoid
    hidden = (silu * up).astype(bf16)
    grad_buffer[slot, 2, :, :D] = dot_tn(hidden, low).astype(bf16)
    up_grad = (hidden_grad * silu).astype(bf16)
    grad_buffer[slot, 1, :, :D] = dot_tn(up_grad, normed).astype(bf16)
    gate_grad = (hidden_grad * up * sigmoid * (1.0 + gate * (1.0 - sigmoid))).astype(bf16)
    grad_buffer[slot, 0, :, :D] = dot_tn(gate_grad, normed).astype(bf16)
    for p in range(n_pieces):

        @pl.when(step == p)
        def _(p=p):
            store(p).start()

    normal_ref[...] += dot_nn(gate_grad, buffer[slot, 0, :, :D]) + dot_nn(
        up_grad, buffer[slot, 1, :, :D]
    )

    @pl.when(step == n_pieces - 1)
    def _():
        for p in range(max(0, n_pieces - 2), n_pieces):
            store(p).wait()


def ffn_backward(upstream, normed, gate, up, pieces):
    rows = upstream.shape[0]
    n_pieces, units = len(pieces), pieces[0].shape[1]
    tile = pl.BlockSpec((rows, units), lambda p: (0, p))
    result = pl.pallas_call(
        functools.partial(ffn_backward_body, n_pieces),
        grid=(n_pieces,),
        in_specs=[whole((rows, D)), whole((rows, D)), tile, tile] + [any_spec()] * n_pieces,
        out_specs=[any_spec()] * n_pieces + [whole((rows, D))],
        out_shape=[jax.ShapeDtypeStruct((3, units, LANES), bf16)] * n_pieces
        + [jax.ShapeDtypeStruct((rows, D), f32)],
        scratch_shapes=[
            pltpu.VMEM((rows, D), bf16),
            pltpu.VMEM((2, 3, units, LANES), bf16),
            pltpu.VMEM((2, 3, units, LANES), bf16),
            pltpu.SemaphoreType.DMA((2,)),
            pltpu.SemaphoreType.DMA((2,)),
        ],
        compiler_params=compiler_params(),
        name="ffn_backward",
    )(upstream, normed, gate, up, *pieces)
    return result[:n_pieces], result[n_pieces]


def mask_bias(key_info, query_info, local_len, half_keys):
    parts = []
    for side in range(2):
        count = half_keys * (side + 1)
        token, segment = key_info[:count, 0:1], key_info[:count, 1:2]
        span = slice(side * local_len, (side + 1) * local_len)
        q_token, q_segment = query_info[0:1, span], query_info[1:2, span]
        parts.append(jnp.where((segment == q_segment) & (token <= q_token), 0.0, neg_large))
    return parts


def attention_forward_body(
    q_ref, kv_ref, key_info, query_info, o_ref, lse_ref, qs, ks, vts, os, bias_low, bias_high
):
    rows = q_ref.shape[0]
    local_len, half_keys = rows // 2, kv_ref.shape[0] // 2
    bias_low[...], bias_high[...] = mask_bias(
        key_info[...], query_info[...], local_len, half_keys
    )
    for h in range(HEADS):
        qs[h] = q_ref[:, h * HEAD_DIM : (h + 1) * HEAD_DIM]
    for h in range(KV_HEADS):
        ks[h] = kv_ref[:, h * HEAD_DIM : (h + 1) * HEAD_DIM]
        value = kv_ref[:, KV_WIDTH + h * HEAD_DIM : KV_WIDTH + (h + 1) * HEAD_DIM]
        vts[h] = value.astype(f32).T.astype(bf16)

    def group(g, carry):
        for i in range(GROUP):
            h = g * GROUP + i
            for side, bias in enumerate((bias_low, bias_high)):
                count = half_keys * (side + 1)
                span = slice(side * local_len, (side + 1) * local_len)
                scores = dot_nt(ks[g, :count], qs[h, span]) * HEAD_DIM**-0.5 + bias[...]
                top = jnp.max(scores, 0, keepdims=True)
                probs = jnp.exp(scores - top)
                total = jnp.sum(probs, 0, keepdims=True)
                out = dot_nn(vts[g, :, :count], probs.astype(bf16)) / total
                os[h, span] = out.T.astype(bf16)
                lse_ref[h, :, span] = top + jnp.log(total)
        return carry

    lax.fori_loop(0, KV_HEADS, group, 0)
    for h in range(HEADS):
        o_ref[:, h * HEAD_DIM : (h + 1) * HEAD_DIM] = os[h]


def attention_forward(query, kv, key_info, query_info):
    rows, keys = query.shape[0], kv.shape[0]
    return pl.pallas_call(
        attention_forward_body,
        out_shape=[
            jax.ShapeDtypeStruct((rows, Q_WIDTH), bf16),
            jax.ShapeDtypeStruct((HEADS, 1, rows), f32),
        ],
        scratch_shapes=[
            pltpu.VMEM((HEADS, rows, HEAD_DIM), bf16),
            pltpu.VMEM((KV_HEADS, keys, HEAD_DIM), bf16),
            pltpu.VMEM((KV_HEADS, HEAD_DIM, keys), bf16),
            pltpu.VMEM((HEADS, rows, HEAD_DIM), bf16),
            pltpu.VMEM((keys // 2, rows // 2), f32),
            pltpu.VMEM((keys, rows // 2), f32),
        ],
        compiler_params=compiler_params(),
        name="attention_forward",
    )(query, kv, key_info, query_info)


def attention_backward_body(
    q_ref, kv_ref, og_ref, lse_ref, key_info, query_info, dq_ref, dkv_ref,
    qs, gs, ks, kts, vs, dqs, dks, dvs, bias_low, bias_high,
):
    rows = q_ref.shape[0]
    local_len, half_keys = rows // 2, kv_ref.shape[0] // 2
    bias_low[...], bias_high[...] = mask_bias(
        key_info[...], query_info[...], local_len, half_keys
    )
    for h in range(HEADS):
        qs[h] = q_ref[:, h * HEAD_DIM : (h + 1) * HEAD_DIM]
        gs[h] = og_ref[:, h * HEAD_DIM : (h + 1) * HEAD_DIM]
    for h in range(KV_HEADS):
        key = kv_ref[:, h * HEAD_DIM : (h + 1) * HEAD_DIM]
        ks[h] = key
        kts[h] = key.astype(f32).T.astype(bf16)
        vs[h] = kv_ref[:, KV_WIDTH + h * HEAD_DIM : KV_WIDTH + (h + 1) * HEAD_DIM]

    def group(g, carry):
        for i in range(GROUP):
            h = g * GROUP + i
            for side, bias in enumerate((bias_low, bias_high)):
                count = half_keys * (side + 1)
                span = slice(side * local_len, (side + 1) * local_len)
                query, grad = qs[h, span], gs[h, span]
                scores = dot_nt(ks[g, :count], query) * HEAD_DIM**-0.5 + bias[...]
                probs = jnp.exp(scores - lse_ref[h, :, span])
                prob_grad = dot_nt(vs[g, :count], grad)
                delta = jnp.sum(probs * prob_grad, 0, keepdims=True)
                score_grad = (probs * (prob_grad - delta)).astype(bf16)
                value_part = dot_nn(probs.astype(bf16), grad)
                key_part = dot_nn(score_grad, query)
                dqs[h, span] = dot_nn(kts[g, :, :count], score_grad).T * HEAD_DIM**-0.5
                if i == 0 and side == 0:
                    dks[g, :count] = key_part
                    dvs[g, :count] = value_part
                    dks[g, count:] = jnp.zeros_like(key_part)
                    dvs[g, count:] = jnp.zeros_like(value_part)
                else:
                    dks[g, :count] += key_part
                    dvs[g, :count] += value_part
        return carry

    lax.fori_loop(0, KV_HEADS, group, 0)
    for h in range(HEADS):
        dq_ref[:, h * HEAD_DIM : (h + 1) * HEAD_DIM] = dqs[h]
    for h in range(KV_HEADS):
        dkv_ref[:, h * HEAD_DIM : (h + 1) * HEAD_DIM] = dks[h] * HEAD_DIM**-0.5
        dkv_ref[:, KV_WIDTH + h * HEAD_DIM : KV_WIDTH + (h + 1) * HEAD_DIM] = dvs[h]


def attention_backward(query, kv, out_grad, lse, key_info, query_info):
    rows, keys = query.shape[0], kv.shape[0]
    return pl.pallas_call(
        attention_backward_body,
        out_shape=[
            jax.ShapeDtypeStruct((rows, Q_WIDTH), f32),
            jax.ShapeDtypeStruct((keys, 2 * KV_WIDTH), f32),
        ],
        scratch_shapes=[
            pltpu.VMEM((HEADS, rows, HEAD_DIM), bf16),
            pltpu.VMEM((HEADS, rows, HEAD_DIM), bf16),
            pltpu.VMEM((KV_HEADS, keys, HEAD_DIM), bf16),
            pltpu.VMEM((KV_HEADS, HEAD_DIM, keys), bf16),
            pltpu.VMEM((KV_HEADS, keys, HEAD_DIM), bf16),
            pltpu.VMEM((HEADS, rows, HEAD_DIM), f32),
            pltpu.VMEM((KV_HEADS, keys, HEAD_DIM), f32),
            pltpu.VMEM((KV_HEADS, keys, HEAD_DIM), f32),
            pltpu.VMEM((keys // 2, rows // 2), f32),
            pltpu.VMEM((keys, rows // 2), f32),
        ],
        compiler_params=compiler_params(),
        name="attention_backward",
    )(query, kv, out_grad, lse, key_info, query_info)


def join_body(moves, n_in, n_out, *refs):
    sources, targets = refs[:n_in], refs[n_in : n_in + n_out]
    buffers, in_sems, out_sems = refs[n_in + n_out : -2], refs[-2], refs[-1]
    loads, stores = [], []
    for m, (i, start, size, o, place) in enumerate(moves):
        run = pl.ds(place, size)
        source = sources[i].at[:, pl.ds(start, size)]
        loads.append(pltpu.make_async_copy(source, buffers[o].at[:, run], in_sems.at[m]))
        stores.append(
            pltpu.make_async_copy(buffers[o].at[:, run], targets[o].at[:, run], out_sems.at[m])
        )
    for load in loads:
        load.start()
    for load, store in zip(loads, stores):
        load.wait()
        store.start()
    for store in stores:
        store.wait()


def join(groups):
    sources, moves, shapes = [], [], []
    for o, group in enumerate(groups):
        place = 0
        for array, start, size in group:
            index = next((i for i, known in enumerate(sources) if known is array), None)
            if index is None:
                index = len(sources)
                sources.append(array)
            moves.append((index, start, size, o, place))
            place += size
        shapes.append((3, place, LANES))
    if any(size % 16 for _, _, size, _, _ in moves):
        return [
            jnp.concatenate([array[:, start : start + size] for array, start, size in group], 1)
            for group in groups
        ]
    return pl.pallas_call(
        functools.partial(join_body, moves, len(sources), len(groups)),
        in_specs=[any_spec()] * len(sources),
        out_specs=[any_spec()] * len(groups),
        out_shape=[jax.ShapeDtypeStruct(shape, bf16) for shape in shapes],
        scratch_shapes=[pltpu.VMEM(shape, bf16) for shape in shapes]
        + [pltpu.SemaphoreType.DMA((len(moves),))] * 2,
        compiler_params=compiler_params(),
        name="join",
    )(*sources)


def exchange(value, dp_xor=0, ctx_xor=0):
    n_dp, n_ctx = lax.axis_size("dp"), lax.axis_size("ctx")
    pairs = [
        (d * n_ctx + c, (d ^ dp_xor) * n_ctx + (c ^ ctx_xor))
        for d in range(n_dp)
        for c in range(n_ctx)
    ]
    return lax.ppermute(value, AXES, pairs)


def dp_bits(color):
    n_dp = lax.axis_size("dp")
    high = [1 << i for i in range(1, n_dp.bit_length() - 1)]
    return (high[::-1] if color else high) + [1]


def bit_set(axis_name, bit):
    return (lax.axis_index(axis_name) & bit) != 0


class Job:
    def __init__(self, chain):
        self.chain = chain
        self.result = None
        self.pending = next(chain)

    def step(self, arrived):
        try:
            self.pending = self.chain.send(arrived)
        except StopIteration as stop:
            self.pending, self.result = None, stop.value


def fence(values, *jobs):
    live = [job for job in jobs if job.pending is not None]
    values, arrived = lax.optimization_barrier((values, [job.pending for job in live]))
    for job, arrays in zip(live, arrived):
        job.step(arrays)
    return values


def finish(values, *jobs):
    while any(job.pending is not None for job in jobs):
        values = fence(values, *jobs)
    return values


def ctx_ordered(parts):
    n = len(parts)
    for i in range(n.bit_length() - 1):
        flag = bit_set("ctx", 1 << i)
        parts = [jnp.where(flag, parts[k ^ (1 << i)], parts[k]) for k in range(n)]
    return parts


def ctx_stage(value):
    return [exchange(value, ctx_xor=k) for k in range(1, lax.axis_size("ctx"))]


def ffn_block(flat):
    block = flat.reshape(-1, 3, D)
    return jnp.pad(block, ((0, 0), (0, 0), (0, LANES - D))).transpose(1, 0, 2)


def gather_ffn_job(block):
    half = block.shape[1] // 2
    (block,) = yield [block]
    parts = [block] + (yield ctx_stage(block))
    sides = join([[(p, 0, half) for p in parts], [(p, half, half) for p in parts]])
    orders = [dp_bits(color) for color in range(2)]
    for i in range(len(orders[0])):
        arrived = yield [exchange(s, dp_xor=order[i]) for s, order in zip(sides, orders)]
        if i + 1 < len(orders[0]):
            size = sides[0].shape[1]
            sides = join([[(s, 0, size), (a, 0, size)] for s, a in zip(sides, arrived)])
    return [sides[0], arrived[0], sides[1], arrived[1]]


def scatter_ffn_job(pieces, shard_len):
    orders = [dp_bits(color)[::-1] for color in range(2)]
    keeps, sends = [pieces[0], pieces[2]], [pieces[1], pieces[3]]
    n_ctx = lax.axis_size("ctx")

    def part_sums(count):
        size = keeps[0].shape[1] // count
        runs = [slice(i * size, (i + 1) * size) for i in range(count)]
        return [
            [
                (k[:, run].astype(f32) + a[:, run].astype(f32)).astype(bf16)
                for k, a in zip(keeps, arrived)
            ]
            for run in runs
        ]

    for i in range(len(orders[0])):
        arrived = yield [exchange(s, dp_xor=order[i]) for s, order in zip(sends, orders)]
        if i + 1 < len(orders[0]):
            keeps, sends = part_sums(2)
    parts = [jnp.concatenate(pair, 1) for pair in part_sums(n_ctx)]
    arrived = yield [exchange(parts[k], ctx_xor=k) for k in range(1, n_ctx)]
    shard = parts[0].astype(f32)
    for part in arrived:
        shard = shard + part.astype(f32)
    return shard[:, :, :D].transpose(1, 0, 2).reshape(shard_len)


def padded(rows):
    return -(-(rows + 1) // 16) * 16


def add_row(block, row):
    rows, cols = block.shape
    extra = jnp.pad(row[None], ((0, padded(rows) - rows - 1), (0, cols - row.shape[0])))
    return jnp.concatenate([block, extra], 0)


def by_rows(shard_len):
    return shard_len % QKV_WIDTH == 0


def gather_attention_job(qkv_flat, out_flat, gain_flat):
    n_dp, n_ctx = lax.axis_size("dp"), lax.axis_size("ctx")
    n, n_bits = n_dp * n_ctx, n_dp.bit_length() - 1
    gain_len = gain_flat.shape[0]
    rows = qkv_flat.shape[0] // math.gcd(qkv_flat.shape[0], QKV_WIDTH)
    if by_rows(qkv_flat.shape[0]):
        qkv, out = qkv_flat.reshape(-1, QKV_WIDTH), out_flat.reshape(-1, D)
        blocks = [add_row(qkv[:, :QK_WIDTH], gain_flat)]
        blocks += [add_row(jnp.concatenate([out, qkv[:, QK_WIDTH:]], 1), gain_flat)]
        (both,) = yield [jnp.concatenate(blocks, 1)]
        parts = ctx_ordered([both] + (yield ctx_stage(both)))
        sides = [[p[:, :QK_WIDTH] for p in parts], [p[:, QK_WIDTH:] for p in parts]]
    else:
        qkv_cols = math.gcd(qkv_flat.shape[0], QKV_WIDTH)
        out_cols = math.gcd(out_flat.shape[0], D)
        blocks = [add_row(qkv_flat.reshape(-1, qkv_cols), gain_flat)]
        blocks += [out_flat.reshape(-1, out_cols)]
        blocks = yield blocks
        arrived = yield ctx_stage(blocks[0]) + ctx_stage(blocks[1])
        sides = [
            ctx_ordered([blocks[0]] + arrived[: n_ctx - 1]),
            ctx_ordered([blocks[1]] + arrived[n_ctx - 1 :]),
        ]
    sides = [jnp.stack(p, 0).reshape((1,) * n_bits + (n_ctx,) + p[0].shape) for p in sides]
    orders = [dp_bits(color) for color in range(2)]
    for i in range(n_bits):
        arrived = yield [exchange(s, dp_xor=order[i]) for s, order in zip(sides, orders)]
        joined = []
        for mine, other, order in zip(sides, arrived, orders):
            flag = bit_set("dp", order[i])
            pair = [jnp.where(flag, other, mine), jnp.where(flag, mine, other)]
            joined.append(jnp.concatenate(pair, n_bits - order[i].bit_length()))
        sides = joined
    first, second = (s.reshape((n,) + s.shape[-2:]) for s in sides)
    gains = first[:, rows, :gain_len].reshape(n * gain_len).astype(f32)
    if by_rows(qkv_flat.shape[0]):
        w_qk = first[:, :rows].reshape(D, QK_WIDTH)
        second = second[:, :rows].reshape(D, QK_WIDTH)
        w_out, w_v = second[:, :D], second[:, D:]
    else:
        w_qkv = first[:, :rows].reshape(D, QKV_WIDTH)
        w_qk, w_v = w_qkv[:, :QK_WIDTH], w_qkv[:, QK_WIDTH:]
        w_out = second.reshape(Q_WIDTH, D)
    return w_qk, w_v, w_out, gains[:D], gains[D:]


def scatter_attention_job(dw_qk, dw_ov, gain_grad, qkv_len, out_len):
    n_dp, n_ctx = lax.axis_size("dp"), lax.axis_size("ctx")
    n, n_bits = n_dp * n_ctx, n_dp.bit_length() - 1
    gain_len = gain_grad.shape[0] // n
    gain_row = gain_grad.astype(bf16).reshape(n, 1, gain_len)

    rows = qkv_len // math.gcd(qkv_len, QKV_WIDTH)

    def with_gain(blocks):
        extra = ((0, 0), (0, padded(rows) - rows - 1), (0, blocks.shape[2] - gain_len))
        return jnp.concatenate([blocks, jnp.pad(gain_row, extra)], 1)

    def with_zeros(blocks):
        return jnp.pad(blocks, ((0, 0), (0, padded(rows) - rows), (0, 0)))

    if by_rows(qkv_len):
        sides = [with_gain(dw_qk.reshape(n, -1, QK_WIDTH)), with_zeros(dw_ov.reshape(n, -1, QK_WIDTH))]
    else:
        dw_qkv = jnp.concatenate([dw_qk, dw_ov[:, Q_WIDTH:]], 1)
        sides = [with_gain(dw_qkv.reshape(n, -1, math.gcd(qkv_len, QKV_WIDTH)))]
        sides += [dw_ov[:, :Q_WIDTH].reshape(n, -1, math.gcd(out_len, D))]
    sides = [s.reshape((2,) * n_bits + (n_ctx,) + s.shape[1:]) for s in sides]
    orders = [dp_bits(color)[::-1] for color in range(2)]
    for i in range(n_bits):
        keeps, sends = [], []
        for side, order in zip(sides, orders):
            low, high = jnp.split(side, 2, n_bits - order[i].bit_length())
            flag = bit_set("dp", order[i])
            keeps.append(jnp.where(flag, high, low))
            sends.append(jnp.where(flag, low, high))
        arrived = yield [exchange(s, dp_xor=order[i]) for s, order in zip(sends, orders)]
        sides = [(k.astype(f32) + a.astype(f32)).astype(bf16) for k, a in zip(keeps, arrived)]
    parts = [ctx_ordered(list(s.reshape((n_ctx,) + s.shape[-2:]))) for s in sides]
    arrived = yield [exchange(p[k], ctx_xor=k) for p in parts for k in range(1, n_ctx)]
    totals = []
    for i in range(2):
        total = parts[i][0].astype(f32)
        for part in arrived[i * (n_ctx - 1) : (i + 1) * (n_ctx - 1)]:
            total = total + part.astype(f32)
        totals.append(total)
    first, second = totals
    gain_part = first[rows, :gain_len]
    if by_rows(qkv_len):
        qkv_part = jnp.concatenate([first[:rows], second[:rows, D:]], 1)
        out_part = second[:rows, :D]
    else:
        qkv_part, out_part = first[:rows], second
    return qkv_part.reshape(qkv_len), out_part.reshape(out_len), gain_part


def low_side():
    return lax.axis_index("ctx") < lax.axis_size("ctx") // 2


def pair_tokens_job(value, wire):
    low = low_side()
    keep = jnp.where(low, value[0], value[1])
    send = jnp.where(low, value[1], value[0]).astype(wire)
    (send,) = yield [send]
    (other,) = yield [exchange(send, ctx_xor=lax.axis_size("ctx") - 1)]
    other = other.astype(value.dtype)
    return jnp.stack([jnp.where(low, keep, other), jnp.where(low, other, keep)], 0)


def gather_group(value):
    n = lax.axis_size("ctx") // 2
    parts = [value] + [exchange(value, ctx_xor=k) for k in range(1, n)]
    return jnp.concatenate([p[0] for p in parts] + [p[1] for p in parts], 0)


def scatter_group(value):
    n = lax.axis_size("ctx") // 2
    parts = value.reshape((2, n, value.shape[0] // (2 * n)) + value.shape[1:])
    result = parts[:, 0].astype(f32)
    for k in range(1, n):
        result = result + exchange(parts[:, k].astype(bf16), ctx_xor=k).astype(f32)
    return result


def per_device(
    inputs, segments, positions, qkv_weights, out_weights, ffn_weights, norm_gains, cotangent
):
    seq_count, local_len, _ = inputs.shape
    assert seq_count == 2
    n_ctx = lax.axis_size("ctx")
    rows = 2 * local_len
    qkv_len, out_len, ffn_len = qkv_weights.shape[1], out_weights.shape[1], ffn_weights.shape[1]

    tokens = Job(pair_tokens_job(inputs, bf16))
    upstream = Job(pair_tokens_job(cotangent, bf16))
    info = Job(pair_tokens_job(jnp.stack([segments, positions], 2), jnp.int32))
    attn = [
        Job(gather_attention_job(qkv_weights[i], out_weights[i], norm_gains[i]))
        for i in range(LAYERS)
    ]

    fence((), attn[0], info)
    blocks = [ffn_block(ffn_weights[i]) for i in range(LAYERS)]
    blocks = fence(blocks, attn[0], info, tokens)
    ffn = [Job(gather_ffn_job(block)) for block in blocks]
    fence((), attn[0])
    fence((), attn[0], tokens, ffn[0])
    finish((), attn[0], info, tokens)
    info = info.result

    index = lax.axis_index("ctx")
    early = jnp.minimum(index, n_ctx - 1 - index)
    within = jnp.arange(local_len, dtype=jnp.int32)
    token_own = jnp.stack([early * local_len + within, (n_ctx - 1 - early) * local_len + within])
    segment_own, position_own = info[..., 0], info[..., 1].reshape(rows)
    info_own = jnp.stack([token_own, segment_own], 2)
    key_info = gather_group(info_own)
    query_info = info_own.reshape(rows, 2).T

    frequency = 1.0 / rope_base ** (jnp.arange(0, HEAD_DIM, 2, dtype=f32) / HEAD_DIM)
    angles = position_own[:, None].astype(f32) * frequency
    cosine, sine = jnp.cos(angles), jnp.sin(angles)
    cosine = jnp.tile(cosine, (1, 8))
    sine = jnp.tile(jnp.concatenate([-sine, sine], 1), (1, 4))

    residual = tokens.result.reshape(rows, D)
    saved = []
    for layer in range(LAYERS):
        w_qk, w_v, w_out, gain_one, gain_two = attn[layer].result
        qk, value, normed_one, scale_one = qkv_forward(residual, gain_one, w_qk, w_v, cosine, sine)
        qk, value = fence((qk, value), ffn[layer])
        kv_own = jnp.concatenate([qk[:, Q_WIDTH:], value], 1)
        kv_all = gather_group(kv_own.reshape(2, local_len, 2 * KV_WIDTH))
        if layer == 0:
            qk, kv_all = fence((qk, kv_all), ffn[0], attn[1])
        else:
            qk, kv_all = fence((qk, kv_all), upstream)
        attended, lse = attention_forward(qk, kv_all, key_info, query_info)
        middle = residual + dot_nn(attended, w_out)
        if layer == 0:
            middle = fence(middle, ffn[1], attn[1])
            middle = fence(middle, ffn[0])
            middle = fence(middle, ffn[0], attn[1])
        else:
            middle = fence(middle, ffn[1], upstream)
        middle = finish(middle, ffn[layer])
        following, normed_two, scale_two, gate, up = ffn_forward(
            middle, gain_two, ffn[layer].result
        )
        saved.append(
            (residual, scale_one, normed_one, qk, kv_all, lse, attended)
            + (middle, scale_two, normed_two, gate, up)
        )
        residual = following
        if layer == 0:
            residual = fence(residual, attn[1], ffn[1])
            residual = finish(residual, attn[1])
    residual = finish(residual, upstream)
    back = Job(pair_tokens_job(residual.reshape(2, local_len, D), bf16))
    gradient = upstream.result.reshape(rows, D)

    attn_jobs, ffn_jobs = [None] * LAYERS, [None] * LAYERS
    for layer in reversed(range(LAYERS)):
        w_qk, w_v, w_out, gain_one, gain_two = attn[layer].result
        residual, scale_one, normed_one, qk, kv_all, lse, attended = saved[layer][:7]
        middle, scale_two, normed_two, gate, up = saved[layer][7:]
        terms, normal_two = ffn_backward(gradient, normed_two, gate, up, ffn[layer].result)
        if layer:
            terms, normal_two = fence((terms, normal_two))
        else:
            terms, normal_two = fence((terms, normal_two), attn_jobs[1])
        ffn_jobs[layer] = Job(scatter_ffn_job(terms, ffn_len))
        gain_two_grad = jnp.sum(normal_two * middle * scale_two, 0)
        gradient = gradient + norm_back(normal_two, middle, scale_two, gain_two)
        attn_low = gradient.astype(bf16)
        attended_grad = dot_nt(attn_low, w_out).astype(bf16)
        if layer:
            attended_grad = fence(attended_grad, ffn_jobs[1], back)
        else:
            attended_grad = fence(attended_grad, ffn_jobs[0], attn_jobs[1], ffn_jobs[1])
        query_grad, kv_grad = attention_backward(
            qk, kv_all, attended_grad, lse, key_info, query_info
        )
        if layer:
            query_grad, kv_grad = fence((query_grad, kv_grad), back)
            kv_grad = scatter_group(kv_grad).reshape(rows, 2 * KV_WIDTH)
            query_grad, kv_grad = fence((query_grad, kv_grad), ffn_jobs[1])
        else:
            query_grad, kv_grad = fence((query_grad, kv_grad))
            kv_grad = scatter_group(kv_grad).reshape(rows, 2 * KV_WIDTH)
            query_grad, kv_grad = fence((query_grad, kv_grad), ffn_jobs[0], attn_jobs[1])
        dw_qk, dw_ov, gain_one_grad, gradient = qkv_backward(
            query_grad, kv_grad, residual, normed_one, scale_one, gain_one, w_qk, w_v,
            cosine, sine, gradient, attended, attn_low,
        )
        if layer:
            dw_qk, dw_ov, gradient = fence((dw_qk, dw_ov, gradient), ffn_jobs[1])
        else:
            dw_qk, dw_ov, gradient = fence((dw_qk, dw_ov, gradient))
        attn_jobs[layer] = Job(
            scatter_attention_job(
                dw_qk, dw_ov, jnp.concatenate([gain_one_grad[0], gain_two_grad]), qkv_len, out_len
            )
        )
    last = Job(pair_tokens_job(gradient.reshape(2, local_len, D), bf16))
    fence((), last)
    fence((), ffn_jobs[0], attn_jobs[0], attn_jobs[1])
    fence((), attn_jobs[0], last)
    fence((), attn_jobs[0], ffn_jobs[0])
    finish((), back, last, *ffn_jobs, *attn_jobs)
    return (
        back.result,
        last.result,
        jnp.stack([job.result[0] for job in attn_jobs]),
        jnp.stack([job.result[1] for job in attn_jobs]),
        jnp.stack([job.result for job in ffn_jobs]),
        jnp.stack([job.result[2] for job in attn_jobs]),
    )


def solution(mesh):
    tokens = P("dp", "ctx", None)
    shards = P(None, ("dp", "ctx"))
    return jax.shard_map(
        per_device,
        mesh=mesh,
        in_specs=(tokens, P("dp", "ctx"), P("dp", "ctx"), shards, shards, shards, shards, tokens),
        out_specs=(tokens, tokens, shards, shards, shards, shards),
        check_vma=False,
    )
```

```python
import functools
import math

import jax
import jax.numpy as jnp
from jax import lax
from jax.experimental import pallas as pl
from jax.experimental.pallas import tpu as pltpu
from jax.sharding import PartitionSpec as P

D = 960
HEADS = 15
KV_HEADS = 5
GROUP = HEADS // KV_HEADS
HEAD_DIM = 64
FF = 2560
LAYERS = 2
Q_WIDTH = HEADS * HEAD_DIM
KV_WIDTH = KV_HEADS * HEAD_DIM
QKV_WIDTH = Q_WIDTH + 2 * KV_WIDTH
QK_WIDTH = Q_WIDTH + KV_WIDTH
LANES = 1024
AXES = ("dp", "ctx")

epsilon = 1e-05
rope_base = 10000.0
neg_large = -1e30
bf16 = jnp.bfloat16
f32 = jnp.float32


def dot_nn(a, b):
    return lax.dot_general(a, b, (((1,), (0,)), ((), ())), preferred_element_type=f32)


def dot_nt(a, b):
    return lax.dot_general(a, b, (((1,), (1,)), ((), ())), preferred_element_type=f32)


def dot_tn(a, b):
    return lax.dot_general(a, b, (((0,), (0,)), ((), ())), preferred_element_type=f32)


def norm_back(upstream, residual, scale_row, gain_row):
    scaled = upstream * gain_row
    return scale_row * scaled - residual * scale_row**3 * jnp.mean(
        scaled * residual, -1, keepdims=True
    )


def compiler_params():
    return pltpu.CompilerParams(vmem_limit_bytes=56 * 1024 * 1024)


def whole(shape):
    return pl.BlockSpec(shape, lambda *_: (0,) * len(shape))


def any_spec():
    return pl.BlockSpec(memory_space=pl.ANY)


def partner(value):
    half = HEAD_DIM // 2
    width = value.shape[1]
    lane = lax.broadcasted_iota(jnp.int32, value.shape, 1) % HEAD_DIM
    return jnp.where(
        lane < half, pltpu.roll(value, width - half, axis=1), pltpu.roll(value, half, axis=1)
    )


def qkv_forward_body(
    x_ref, gain_ref, qk_ref, v_ref, cos_ref, sin_ref, qk_out, v_out, normed_ref, scale_ref
):
    x = x_ref[...]
    scale = lax.rsqrt(jnp.mean(x * x, -1, keepdims=True) + epsilon)
    scale_ref[...] = scale
    normed = (x * scale * gain_ref[...]).astype(bf16)
    normed_ref[...] = normed
    block = cos_ref.shape[1]
    for j in range(QK_WIDTH // block):
        span = slice(j * block, (j + 1) * block)
        part = dot_nn(normed, qk_ref[:, span])
        qk_out[:, span] = (part * cos_ref[...] + partner(part) * sin_ref[...]).astype(bf16)
    v_out[...] = dot_nn(normed, v_ref[...]).astype(bf16)


def qkv_forward(x, gain, w_qk, w_v, cosine, sine):
    rows = x.shape[0]
    return pl.pallas_call(
        qkv_forward_body,
        out_shape=[
            jax.ShapeDtypeStruct((rows, QK_WIDTH), bf16),
            jax.ShapeDtypeStruct((rows, KV_WIDTH), bf16),
            jax.ShapeDtypeStruct((rows, D), bf16),
            jax.ShapeDtypeStruct((rows, 1), f32),
        ],
        compiler_params=compiler_params(),
        name="qkv_forward",
    )(x, gain[None], w_qk, w_v, cosine, sine)


def qkv_backward_body(
    dq_ref, dkv_ref, x_ref, normed_ref, scale_ref, gain_ref, qk_ref, v_ref, cos_ref, sin_ref,
    upstream_ref, attended_ref, low_ref, dqk_w, dov_w, dgain_ref, dx_ref, pre, low,
):
    pre[:, :Q_WIDTH] = dq_ref[...]
    pre[:, Q_WIDTH:] = dkv_ref[:, :KV_WIDTH]
    block = cos_ref.shape[1]
    normed = normed_ref[...]
    for j in range(QK_WIDTH // block):
        span = slice(j * block, (j + 1) * block)
        part = pre[:, span]
        back = (part * cos_ref[...] - partner(part) * sin_ref[...]).astype(bf16)
        low[:, span] = back
        dqk_w[:, span] = dot_tn(normed, back).astype(bf16)
    dv = dkv_ref[:, KV_WIDTH:].astype(bf16)
    dov_w[:, :Q_WIDTH] = dot_tn(attended_ref[...], low_ref[...]).astype(bf16)
    dov_w[:, Q_WIDTH:] = dot_tn(normed, dv).astype(bf16)
    normal = dot_nt(low[...], qk_ref[...]) + dot_nt(dv, v_ref[...])
    x = x_ref[...]
    scale = scale_ref[...]
    dgain_ref[...] = jnp.sum(normal * x * scale, 0, keepdims=True)
    dx_ref[...] = upstream_ref[...] + norm_back(normal, x, scale, gain_ref[...])


def qkv_backward(
    dq, dkv, x, normed, scale, gain, w_qk, w_v, cosine, sine, upstream, attended, low
):
    rows = x.shape[0]
    return pl.pallas_call(
        qkv_backward_body,
        out_shape=[
            jax.ShapeDtypeStruct((D, QK_WIDTH), bf16),
            jax.ShapeDtypeStruct((Q_WIDTH, QK_WIDTH), bf16),
            jax.ShapeDtypeStruct((1, D), f32),
            jax.ShapeDtypeStruct((rows, D), f32),
        ],
        scratch_shapes=[pltpu.VMEM((rows, QK_WIDTH), f32), pltpu.VMEM((rows, QK_WIDTH), bf16)],
        compiler_params=compiler_params(),
        name="qkv_backward",
    )(dq, dkv, x, normed, scale, gain[None], w_qk, w_v, cosine, sine, upstream, attended, low)


def ffn_forward_body(n_pieces, *refs):
    middle_ref, gain_ref = refs[:2]
    pieces = refs[2 : 2 + n_pieces]
    out_ref, normed_ref, scale_ref, gate_ref, up_ref, buffer, sems = refs[2 + n_pieces :]
    step = pl.program_id(0)

    def load(p):
        return pltpu.make_async_copy(pieces[p], buffer.at[p % 2], sems.at[p % 2])

    @pl.when(step == 0)
    def _():
        load(0).start()
        middle = middle_ref[...]
        scale = lax.rsqrt(jnp.mean(middle * middle, -1, keepdims=True) + epsilon)
        scale_ref[...] = scale
        normed_ref[...] = (middle * scale * gain_ref[...]).astype(bf16)
        out_ref[...] = middle

    for p in range(n_pieces):

        @pl.when(step == p)
        def _(p=p):
            if p + 1 < n_pieces:
                load(p + 1).start()
            load(p).wait()

    slot = step % 2
    normed = normed_ref[...]
    gate = dot_nt(normed, buffer[slot, 0, :, :D])
    up = dot_nt(normed, buffer[slot, 1, :, :D])
    gate_ref[...] = gate
    up_ref[...] = up
    hidden = (gate / (1.0 + jnp.exp(-gate)) * up).astype(bf16)
    out_ref[...] += dot_nn(hidden, buffer[slot, 2, :, :D])


def ffn_forward(middle, gain, pieces):
    rows = middle.shape[0]
    n_pieces, units = len(pieces), pieces[0].shape[1]
    tile = pl.BlockSpec((rows, units), lambda p: (0, p))
    return pl.pallas_call(
        functools.partial(ffn_forward_body, n_pieces),
        grid=(n_pieces,),
        in_specs=[whole((rows, D)), whole((1, D))] + [any_spec()] * n_pieces,
        out_specs=[whole((rows, D)), whole((rows, D)), whole((rows, 1)), tile, tile],
        out_shape=[
            jax.ShapeDtypeStruct((rows, D), f32),
            jax.ShapeDtypeStruct((rows, D), bf16),
            jax.ShapeDtypeStruct((rows, 1), f32),
            jax.ShapeDtypeStruct((rows, FF), f32),
            jax.ShapeDtypeStruct((rows, FF), f32),
        ],
        scratch_shapes=[pltpu.VMEM((2, 3, units, LANES), bf16), pltpu.SemaphoreType.DMA((2,))],
        compiler_params=compiler_params(),
        name="ffn_forward",
    )(middle, gain[None], *pieces)


def ffn_backward_body(n_pieces, *refs):
    upstream_ref, normed_ref, gate_ref, up_ref = refs[:4]
    pieces = refs[4 : 4 + n_pieces]
    grads = refs[4 + n_pieces : 4 + 2 * n_pieces]
    normal_ref, low_ref, buffer, grad_buffer, sems, out_sems = refs[4 + 2 * n_pieces :]
    step = pl.program_id(0)

    def load(p):
        return pltpu.make_async_copy(pieces[p], buffer.at[p % 2], sems.at[p % 2])

    def store(p):
        return pltpu.make_async_copy(grad_buffer.at[p % 2], grads[p], out_sems.at[p % 2])

    @pl.when(step == 0)
    def _():
        load(0).start()
        low_ref[...] = upstream_ref[...].astype(bf16)
        grad_buffer[:, :, :, D:] = jnp.zeros_like(grad_buffer[:, :, :, D:])
        normal_ref[...] = jnp.zeros_like(normal_ref)

    for p in range(n_pieces):

        @pl.when(step == p)
        def _(p=p):
            if p + 1 < n_pieces:
                load(p + 1).start()
            load(p).wait()
            if p >= 2:
                store(p - 2).wait()

    slot = step % 2
    low = low_ref[...]
    normed = normed_ref[...]
    gate = gate_ref[...]
    up = up_ref[...]
    hidden_grad = dot_nt(low, buffer[slot, 2, :, :D])
    sigmoid = 1.0 / (1.0 + jnp.exp(-gate))
    silu = gate * sigmoid
    hidden = (silu * up).astype(bf16)
    grad_buffer[slot, 2, :, :D] = dot_tn(hidden, low).astype(bf16)
    up_grad = (hidden_grad * silu).astype(bf16)
    grad_buffer[slot, 1, :, :D] = dot_tn(up_grad, normed).astype(bf16)
    gate_grad = (hidden_grad * up * sigmoid * (1.0 + gate * (1.0 - sigmoid))).astype(bf16)
    grad_buffer[slot, 0, :, :D] = dot_tn(gate_grad, normed).astype(bf16)
    for p in range(n_pieces):

        @pl.when(step == p)
        def _(p=p):
            store(p).start()

    normal_ref[...] += dot_nn(gate_grad, buffer[slot, 0, :, :D]) + dot_nn(
        up_grad, buffer[slot, 1, :, :D]
    )

    @pl.when(step == n_pieces - 1)
    def _():
        for p in range(max(0, n_pieces - 2), n_pieces):
            store(p).wait()


def ffn_backward(upstream, normed, gate, up, pieces):
    rows = upstream.shape[0]
    n_pieces, units = len(pieces), pieces[0].shape[1]
    tile = pl.BlockSpec((rows, units), lambda p: (0, p))
    result = pl.pallas_call(
        functools.partial(ffn_backward_body, n_pieces),
        grid=(n_pieces,),
        in_specs=[whole((rows, D)), whole((rows, D)), tile, tile] + [any_spec()] * n_pieces,
        out_specs=[any_spec()] * n_pieces + [whole((rows, D))],
        out_shape=[jax.ShapeDtypeStruct((3, units, LANES), bf16)] * n_pieces
        + [jax.ShapeDtypeStruct((rows, D), f32)],
        scratch_shapes=[
            pltpu.VMEM((rows, D), bf16),
            pltpu.VMEM((2, 3, units, LANES), bf16),
            pltpu.VMEM((2, 3, units, LANES), bf16),
            pltpu.SemaphoreType.DMA((2,)),
            pltpu.SemaphoreType.DMA((2,)),
        ],
        compiler_params=compiler_params(),
        name="ffn_backward",
    )(upstream, normed, gate, up, *pieces)
    return result[:n_pieces], result[n_pieces]


def mask_bias(key_info, query_info, local_len, half_keys):
    parts = []
    for side in range(2):
        count = half_keys * (side + 1)
        token, segment = key_info[:count, 0:1], key_info[:count, 1:2]
        span = slice(side * local_len, (side + 1) * local_len)
        q_token, q_segment = query_info[0:1, span], query_info[1:2, span]
        parts.append(jnp.where((segment == q_segment) & (token <= q_token), 0.0, neg_large))
    return parts


def attention_forward_body(
    q_ref, kv_ref, key_info, query_info, o_ref, lse_ref, qs, ks, vts, os, bias_low, bias_high
):
    rows = q_ref.shape[0]
    local_len, half_keys = rows // 2, kv_ref.shape[0] // 2
    bias_low[...], bias_high[...] = mask_bias(
        key_info[...], query_info[...], local_len, half_keys
    )
    for h in range(HEADS):
        qs[h] = q_ref[:, h * HEAD_DIM : (h + 1) * HEAD_DIM]
    for h in range(KV_HEADS):
        ks[h] = kv_ref[:, h * HEAD_DIM : (h + 1) * HEAD_DIM]
        value = kv_ref[:, KV_WIDTH + h * HEAD_DIM : KV_WIDTH + (h + 1) * HEAD_DIM]
        vts[h] = value.astype(f32).T.astype(bf16)

    def group(g, carry):
        for i in range(GROUP):
            h = g * GROUP + i
            for side, bias in enumerate((bias_low, bias_high)):
                count = half_keys * (side + 1)
                span = slice(side * local_len, (side + 1) * local_len)
                scores = dot_nt(ks[g, :count], qs[h, span]) * HEAD_DIM**-0.5 + bias[...]
                top = jnp.max(scores, 0, keepdims=True)
                probs = jnp.exp(scores - top)
                total = jnp.sum(probs, 0, keepdims=True)
                out = dot_nn(vts[g, :, :count], probs.astype(bf16)) / total
                os[h, span] = out.T.astype(bf16)
                lse_ref[h, :, span] = top + jnp.log(total)
        return carry

    lax.fori_loop(0, KV_HEADS, group, 0)
    for h in range(HEADS):
        o_ref[:, h * HEAD_DIM : (h + 1) * HEAD_DIM] = os[h]


def attention_forward(query, kv, key_info, query_info):
    rows, keys = query.shape[0], kv.shape[0]
    return pl.pallas_call(
        attention_forward_body,
        out_shape=[
            jax.ShapeDtypeStruct((rows, Q_WIDTH), bf16),
            jax.ShapeDtypeStruct((HEADS, 1, rows), f32),
        ],
        scratch_shapes=[
            pltpu.VMEM((HEADS, rows, HEAD_DIM), bf16),
            pltpu.VMEM((KV_HEADS, keys, HEAD_DIM), bf16),
            pltpu.VMEM((KV_HEADS, HEAD_DIM, keys), bf16),
            pltpu.VMEM((HEADS, rows, HEAD_DIM), bf16),
            pltpu.VMEM((keys // 2, rows // 2), f32),
            pltpu.VMEM((keys, rows // 2), f32),
        ],
        compiler_params=compiler_params(),
        name="attention_forward",
    )(query, kv, key_info, query_info)


def attention_backward_body(
    q_ref, kv_ref, og_ref, lse_ref, key_info, query_info, dq_ref, dkv_ref,
    qs, gs, ks, kts, vs, dqs, dks, dvs, bias_low, bias_high,
):
    rows = q_ref.shape[0]
    local_len, half_keys = rows // 2, kv_ref.shape[0] // 2
    bias_low[...], bias_high[...] = mask_bias(
        key_info[...], query_info[...], local_len, half_keys
    )
    for h in range(HEADS):
        qs[h] = q_ref[:, h * HEAD_DIM : (h + 1) * HEAD_DIM]
        gs[h] = og_ref[:, h * HEAD_DIM : (h + 1) * HEAD_DIM]
    for h in range(KV_HEADS):
        key = kv_ref[:, h * HEAD_DIM : (h + 1) * HEAD_DIM]
        ks[h] = key
        kts[h] = key.astype(f32).T.astype(bf16)
        vs[h] = kv_ref[:, KV_WIDTH + h * HEAD_DIM : KV_WIDTH + (h + 1) * HEAD_DIM]

    def group(g, carry):
        for i in range(GROUP):
            h = g * GROUP + i
            for side, bias in enumerate((bias_low, bias_high)):
                count = half_keys * (side + 1)
                span = slice(side * local_len, (side + 1) * local_len)
                query, grad = qs[h, span], gs[h, span]
                scores = dot_nt(ks[g, :count], query) * HEAD_DIM**-0.5 + bias[...]
                probs = jnp.exp(scores - lse_ref[h, :, span])
                prob_grad = dot_nt(vs[g, :count], grad)
                delta = jnp.sum(probs * prob_grad, 0, keepdims=True)
                score_grad = (probs * (prob_grad - delta)).astype(bf16)
                value_part = dot_nn(probs.astype(bf16), grad)
                key_part = dot_nn(score_grad, query)
                dqs[h, span] = dot_nn(kts[g, :, :count], score_grad).T * HEAD_DIM**-0.5
                if i == 0 and side == 0:
                    dks[g, :count] = key_part
                    dvs[g, :count] = value_part
                    dks[g, count:] = jnp.zeros_like(key_part)
                    dvs[g, count:] = jnp.zeros_like(value_part)
                else:
                    dks[g, :count] += key_part
                    dvs[g, :count] += value_part
        return carry

    lax.fori_loop(0, KV_HEADS, group, 0)
    for h in range(HEADS):
        dq_ref[:, h * HEAD_DIM : (h + 1) * HEAD_DIM] = dqs[h]
    for h in range(KV_HEADS):
        dkv_ref[:, h * HEAD_DIM : (h + 1) * HEAD_DIM] = dks[h] * HEAD_DIM**-0.5
        dkv_ref[:, KV_WIDTH + h * HEAD_DIM : KV_WIDTH + (h + 1) * HEAD_DIM] = dvs[h]


def attention_backward(query, kv, out_grad, lse, key_info, query_info):
    rows, keys = query.shape[0], kv.shape[0]
    return pl.pallas_call(
        attention_backward_body,
        out_shape=[
            jax.ShapeDtypeStruct((rows, Q_WIDTH), f32),
            jax.ShapeDtypeStruct((keys, 2 * KV_WIDTH), f32),
        ],
        scratch_shapes=[
            pltpu.VMEM((HEADS, rows, HEAD_DIM), bf16),
            pltpu.VMEM((HEADS, rows, HEAD_DIM), bf16),
            pltpu.VMEM((KV_HEADS, keys, HEAD_DIM), bf16),
            pltpu.VMEM((KV_HEADS, HEAD_DIM, keys), bf16),
            pltpu.VMEM((KV_HEADS, keys, HEAD_DIM), bf16),
            pltpu.VMEM((HEADS, rows, HEAD_DIM), f32),
            pltpu.VMEM((KV_HEADS, keys, HEAD_DIM), f32),
            pltpu.VMEM((KV_HEADS, keys, HEAD_DIM), f32),
            pltpu.VMEM((keys // 2, rows // 2), f32),
            pltpu.VMEM((keys, rows // 2), f32),
        ],
        compiler_params=compiler_params(),
        name="attention_backward",
    )(query, kv, out_grad, lse, key_info, query_info)


def join_body(moves, n_in, n_out, *refs):
    sources, targets = refs[:n_in], refs[n_in : n_in + n_out]
    buffers, in_sems, out_sems = refs[n_in + n_out : -2], refs[-2], refs[-1]
    loads, stores = [], []
    for m, (i, start, size, o, place) in enumerate(moves):
        run = pl.ds(place, size)
        source = sources[i].at[:, pl.ds(start, size)]
        loads.append(pltpu.make_async_copy(source, buffers[o].at[:, run], in_sems.at[m]))
        stores.append(
            pltpu.make_async_copy(buffers[o].at[:, run], targets[o].at[:, run], out_sems.at[m])
        )
    for load in loads:
        load.start()
    for load, store in zip(loads, stores):
        load.wait()
        store.start()
    for store in stores:
        store.wait()


def join(groups):
    sources, moves, shapes = [], [], []
    for o, group in enumerate(groups):
        place = 0
        for array, start, size in group:
            index = next((i for i, known in enumerate(sources) if known is array), None)
            if index is None:
                index = len(sources)
                sources.append(array)
            moves.append((index, start, size, o, place))
            place += size
        shapes.append((3, place, LANES))
    if any(size % 16 for _, _, size, _, _ in moves):
        return [
            jnp.concatenate([array[:, start : start + size] for array, start, size in group], 1)
            for group in groups
        ]
    return pl.pallas_call(
        functools.partial(join_body, moves, len(sources), len(groups)),
        in_specs=[any_spec()] * len(sources),
        out_specs=[any_spec()] * len(groups),
        out_shape=[jax.ShapeDtypeStruct(shape, bf16) for shape in shapes],
        scratch_shapes=[pltpu.VMEM(shape, bf16) for shape in shapes]
        + [pltpu.SemaphoreType.DMA((len(moves),))] * 2,
        compiler_params=compiler_params(),
        name="join",
    )(*sources)


def exchange(value, dp_xor=0, ctx_xor=0):
    n_dp, n_ctx = lax.axis_size("dp"), lax.axis_size("ctx")
    pairs = [
        (d * n_ctx + c, (d ^ dp_xor) * n_ctx + (c ^ ctx_xor))
        for d in range(n_dp)
        for c in range(n_ctx)
    ]
    return lax.ppermute(value, AXES, pairs)


def dp_bits(color):
    n_dp = lax.axis_size("dp")
    high = [1 << i for i in range(1, n_dp.bit_length() - 1)]
    return (high[::-1] if color else high) + [1]


def bit_set(axis_name, bit):
    return (lax.axis_index(axis_name) & bit) != 0


class Job:
    def __init__(self, chain):
        self.chain = chain
        self.result = None
        self.pending = next(chain)

    def step(self, arrived):
        try:
            self.pending = self.chain.send(arrived)
        except StopIteration as stop:
            self.pending, self.result = None, stop.value


def fence(values, *jobs):
    live = [job for job in jobs if job.pending is not None]
    values, arrived = lax.optimization_barrier((values, [job.pending for job in live]))
    for job, arrays in zip(live, arrived):
        job.step(arrays)
    return values


def finish(values, *jobs):
    while any(job.pending is not None for job in jobs):
        values = fence(values, *jobs)
    return values


def ctx_ordered(parts):
    n = len(parts)
    for i in range(n.bit_length() - 1):
        flag = bit_set("ctx", 1 << i)
        parts = [jnp.where(flag, parts[k ^ (1 << i)], parts[k]) for k in range(n)]
    return parts


def ctx_stage(value):
    return [exchange(value, ctx_xor=k) for k in range(1, lax.axis_size("ctx"))]


def ffn_block(flat):
    block = flat.reshape(-1, 3, D)
    return jnp.pad(block, ((0, 0), (0, 0), (0, LANES - D))).transpose(1, 0, 2)


def gather_ffn_job(block):
    (block,) = yield [block]
    parts = [block] + (yield ctx_stage(block))
    units, half = block.shape[1], len(parts) // 2
    sides = join([[(p, 0, units) for p in run] for run in (parts[:half], parts[half:])])
    orders = [dp_bits(color) for color in range(2)]
    for i in range(len(orders[0])):
        arrived = yield [exchange(s, dp_xor=order[i]) for s, order in zip(sides, orders)]
        if i + 1 < len(orders[0]):
            size = sides[0].shape[1]
            sides = join([[(s, 0, size), (a, 0, size)] for s, a in zip(sides, arrived)])
    return [sides[0], arrived[0], sides[1], arrived[1]]


def scatter_ffn_job(pieces, shard_len):
    orders = [dp_bits(color)[::-1] for color in range(2)]
    keeps, sends = [pieces[0], pieces[2]], [pieces[1], pieces[3]]
    n_ctx = lax.axis_size("ctx")

    def part_sums(count):
        size = keeps[0].shape[1] // count
        runs = [slice(i * size, (i + 1) * size) for i in range(count)]
        return [
            [
                (k[:, run].astype(f32) + a[:, run].astype(f32)).astype(bf16)
                for k, a in zip(keeps, arrived)
            ]
            for run in runs
        ]

    for i in range(len(orders[0])):
        arrived = yield [exchange(s, dp_xor=order[i]) for s, order in zip(sends, orders)]
        if i + 1 < len(orders[0]):
            keeps, sends = part_sums(2)
    runs = part_sums(n_ctx // 2)
    parts = [run[0] for run in runs] + [run[1] for run in runs]
    arrived = yield [exchange(parts[k], ctx_xor=k) for k in range(1, n_ctx)]
    shard = parts[0].astype(f32)
    for part in arrived:
        shard = shard + part.astype(f32)
    return shard[:, :, :D].transpose(1, 0, 2).reshape(shard_len)


def padded(rows):
    return -(-(rows + 1) // 16) * 16


def add_row(block, row):
    rows, cols = block.shape
    extra = jnp.pad(row[None], ((0, padded(rows) - rows - 1), (0, cols - row.shape[0])))
    return jnp.concatenate([block, extra], 0)


def by_rows(shard_len):
    return shard_len % QKV_WIDTH == 0


def gather_attention_job(qkv_flat, out_flat, gain_flat):
    n_dp, n_ctx = lax.axis_size("dp"), lax.axis_size("ctx")
    n, n_bits = n_dp * n_ctx, n_dp.bit_length() - 1
    gain_len = gain_flat.shape[0]
    rows = qkv_flat.shape[0] // math.gcd(qkv_flat.shape[0], QKV_WIDTH)
    if by_rows(qkv_flat.shape[0]):
        qkv, out = qkv_flat.reshape(-1, QKV_WIDTH), out_flat.reshape(-1, D)
        blocks = [add_row(qkv[:, :QK_WIDTH], gain_flat)]
        blocks += [add_row(jnp.concatenate([out, qkv[:, QK_WIDTH:]], 1), gain_flat)]
        (both,) = yield [jnp.concatenate(blocks, 1)]
        parts = ctx_ordered([both] + (yield ctx_stage(both)))
        sides = [[p[:, :QK_WIDTH] for p in parts], [p[:, QK_WIDTH:] for p in parts]]
    else:
        qkv_cols = math.gcd(qkv_flat.shape[0], QKV_WIDTH)
        out_cols = math.gcd(out_flat.shape[0], D)
        blocks = [add_row(qkv_flat.reshape(-1, qkv_cols), gain_flat)]
        blocks += [out_flat.reshape(-1, out_cols)]
        blocks = yield blocks
        arrived = yield ctx_stage(blocks[0]) + ctx_stage(blocks[1])
        sides = [
            ctx_ordered([blocks[0]] + arrived[: n_ctx - 1]),
            ctx_ordered([blocks[1]] + arrived[n_ctx - 1 :]),
        ]
    sides = [jnp.stack(p, 0).reshape((1,) * n_bits + (n_ctx,) + p[0].shape) for p in sides]
    orders = [dp_bits(color) for color in range(2)]
    for i in range(n_bits):
        arrived = yield [exchange(s, dp_xor=order[i]) for s, order in zip(sides, orders)]
        joined = []
        for mine, other, order in zip(sides, arrived, orders):
            flag = bit_set("dp", order[i])
            pair = [jnp.where(flag, other, mine), jnp.where(flag, mine, other)]
            joined.append(jnp.concatenate(pair, n_bits - order[i].bit_length()))
        sides = joined
    first, second = (s.reshape((n,) + s.shape[-2:]) for s in sides)
    gains = first[:, rows, :gain_len].reshape(n * gain_len).astype(f32)
    if by_rows(qkv_flat.shape[0]):
        w_qk = first[:, :rows].reshape(D, QK_WIDTH)
        second = second[:, :rows].reshape(D, QK_WIDTH)
        w_out, w_v = second[:, :D], second[:, D:]
    else:
        w_qkv = first[:, :rows].reshape(D, QKV_WIDTH)
        w_qk, w_v = w_qkv[:, :QK_WIDTH], w_qkv[:, QK_WIDTH:]
        w_out = second.reshape(Q_WIDTH, D)
    return w_qk, w_v, w_out, gains[:D], gains[D:]


def scatter_attention_job(dw_qk, dw_ov, gain_grad, qkv_len, out_len):
    n_dp, n_ctx = lax.axis_size("dp"), lax.axis_size("ctx")
    n, n_bits = n_dp * n_ctx, n_dp.bit_length() - 1
    gain_len = gain_grad.shape[0] // n
    gain_row = gain_grad.astype(bf16).reshape(n, 1, gain_len)

    rows = qkv_len // math.gcd(qkv_len, QKV_WIDTH)

    def with_gain(blocks):
        extra = ((0, 0), (0, padded(rows) - rows - 1), (0, blocks.shape[2] - gain_len))
        return jnp.concatenate([blocks, jnp.pad(gain_row, extra)], 1)

    def with_zeros(blocks):
        return jnp.pad(blocks, ((0, 0), (0, padded(rows) - rows), (0, 0)))

    if by_rows(qkv_len):
        sides = [with_gain(dw_qk.reshape(n, -1, QK_WIDTH)), with_zeros(dw_ov.reshape(n, -1, QK_WIDTH))]
    else:
        dw_qkv = jnp.concatenate([dw_qk, dw_ov[:, Q_WIDTH:]], 1)
        sides = [with_gain(dw_qkv.reshape(n, -1, math.gcd(qkv_len, QKV_WIDTH)))]
        sides += [dw_ov[:, :Q_WIDTH].reshape(n, -1, math.gcd(out_len, D))]
    sides = [s.reshape((2,) * n_bits + (n_ctx,) + s.shape[1:]) for s in sides]
    orders = [dp_bits(color)[::-1] for color in range(2)]
    for i in range(n_bits):
        keeps, sends = [], []
        for side, order in zip(sides, orders):
            low, high = jnp.split(side, 2, n_bits - order[i].bit_length())
            flag = bit_set("dp", order[i])
            keeps.append(jnp.where(flag, high, low))
            sends.append(jnp.where(flag, low, high))
        arrived = yield [exchange(s, dp_xor=order[i]) for s, order in zip(sends, orders)]
        sides = [(k.astype(f32) + a.astype(f32)).astype(bf16) for k, a in zip(keeps, arrived)]
    parts = [ctx_ordered(list(s.reshape((n_ctx,) + s.shape[-2:]))) for s in sides]
    arrived = yield [exchange(p[k], ctx_xor=k) for p in parts for k in range(1, n_ctx)]
    totals = []
    for i in range(2):
        total = parts[i][0].astype(f32)
        for part in arrived[i * (n_ctx - 1) : (i + 1) * (n_ctx - 1)]:
            total = total + part.astype(f32)
        totals.append(total)
    first, second = totals
    gain_part = first[rows, :gain_len]
    if by_rows(qkv_len):
        qkv_part = jnp.concatenate([first[:rows], second[:rows, D:]], 1)
        out_part = second[:rows, :D]
    else:
        qkv_part, out_part = first[:rows], second
    return qkv_part.reshape(qkv_len), out_part.reshape(out_len), gain_part


def low_side():
    return lax.axis_index("ctx") < lax.axis_size("ctx") // 2


def pair_tokens_job(value, wire):
    low = low_side()
    keep = jnp.where(low, value[0], value[1])
    send = jnp.where(low, value[1], value[0]).astype(wire)
    (send,) = yield [send]
    (other,) = yield [exchange(send, ctx_xor=lax.axis_size("ctx") - 1)]
    other = other.astype(value.dtype)
    return jnp.stack([jnp.where(low, keep, other), jnp.where(low, other, keep)], 0)


def gather_group(value):
    n = lax.axis_size("ctx") // 2
    parts = [value] + [exchange(value, ctx_xor=k) for k in range(1, n)]
    return jnp.concatenate([p[0] for p in parts] + [p[1] for p in parts], 0)


def scatter_group(value):
    n = lax.axis_size("ctx") // 2
    parts = value.reshape((2, n, value.shape[0] // (2 * n)) + value.shape[1:])
    result = parts[:, 0].astype(f32)
    for k in range(1, n):
        result = result + exchange(parts[:, k].astype(bf16), ctx_xor=k).astype(f32)
    return result


def per_device(
    inputs, segments, positions, qkv_weights, out_weights, ffn_weights, norm_gains, cotangent
):
    seq_count, local_len, _ = inputs.shape
    assert seq_count == 2
    n_ctx = lax.axis_size("ctx")
    rows = 2 * local_len
    qkv_len, out_len, ffn_len = qkv_weights.shape[1], out_weights.shape[1], ffn_weights.shape[1]

    tokens = Job(pair_tokens_job(inputs, bf16))
    upstream = Job(pair_tokens_job(cotangent, bf16))
    info = Job(pair_tokens_job(jnp.stack([segments, positions], 2), jnp.int32))
    attn = [
        Job(gather_attention_job(qkv_weights[i], out_weights[i], norm_gains[i]))
        for i in range(LAYERS)
    ]

    fence((), attn[0], info)
    blocks = [ffn_block(ffn_weights[i]) for i in range(LAYERS)]
    blocks = fence(blocks, attn[0], info, tokens)
    ffn = [Job(gather_ffn_job(block)) for block in blocks]
    fence((), attn[0])
    fence((), attn[0], tokens, ffn[0])
    finish((), attn[0], info, tokens)
    info = info.result

    index = lax.axis_index("ctx")
    early = jnp.minimum(index, n_ctx - 1 - index)
    within = jnp.arange(local_len, dtype=jnp.int32)
    token_own = jnp.stack([early * local_len + within, (n_ctx - 1 - early) * local_len + within])
    segment_own, position_own = info[..., 0], info[..., 1].reshape(rows)
    info_own = jnp.stack([token_own, segment_own], 2)
    key_info = gather_group(info_own)
    query_info = info_own.reshape(rows, 2).T

    frequency = 1.0 / rope_base ** (jnp.arange(0, HEAD_DIM, 2, dtype=f32) / HEAD_DIM)
    angles = position_own[:, None].astype(f32) * frequency
    cosine, sine = jnp.cos(angles), jnp.sin(angles)
    cosine = jnp.tile(cosine, (1, 8))
    sine = jnp.tile(jnp.concatenate([-sine, sine], 1), (1, 4))

    residual = tokens.result.reshape(rows, D)
    saved = []
    for layer in range(LAYERS):
        w_qk, w_v, w_out, gain_one, gain_two = attn[layer].result
        qk, value, normed_one, scale_one = qkv_forward(residual, gain_one, w_qk, w_v, cosine, sine)
        qk, value = fence((qk, value), ffn[layer])
        kv_own = jnp.concatenate([qk[:, Q_WIDTH:], value], 1)
        kv_all = gather_group(kv_own.reshape(2, local_len, 2 * KV_WIDTH))
        if layer == 0:
            qk, kv_all = fence((qk, kv_all), ffn[0], attn[1])
        else:
            qk, kv_all = fence((qk, kv_all), upstream)
        attended, lse = attention_forward(qk, kv_all, key_info, query_info)
        middle = residual + dot_nn(attended, w_out)
        if layer == 0:
            middle = fence(middle, ffn[1], attn[1])
            middle = fence(middle, ffn[0])
            middle = fence(middle, ffn[0], attn[1])
        else:
            middle = fence(middle, ffn[1], upstream)
        middle = finish(middle, ffn[layer])
        following, normed_two, scale_two, gate, up = ffn_forward(
            middle, gain_two, ffn[layer].result
        )
        saved.append(
            (residual, scale_one, normed_one, qk, kv_all, lse, attended)
            + (middle, scale_two, normed_two, gate, up)
        )
        residual = following
        if layer == 0:
            residual = fence(residual, attn[1], ffn[1])
            residual = finish(residual, attn[1])
    residual = finish(residual, upstream)
    back = Job(pair_tokens_job(residual.reshape(2, local_len, D), bf16))
    gradient = upstream.result.reshape(rows, D)

    attn_jobs, ffn_jobs = [None] * LAYERS, [None] * LAYERS
    for layer in reversed(range(LAYERS)):
        w_qk, w_v, w_out, gain_one, gain_two = attn[layer].result
        residual, scale_one, normed_one, qk, kv_all, lse, attended = saved[layer][:7]
        middle, scale_two, normed_two, gate, up = saved[layer][7:]
        terms, normal_two = ffn_backward(gradient, normed_two, gate, up, ffn[layer].result)
        if layer:
            terms, normal_two = fence((terms, normal_two))
        else:
            terms, normal_two = fence((terms, normal_two), attn_jobs[1], ffn_jobs[1])
        ffn_jobs[layer] = Job(scatter_ffn_job(terms, ffn_len))
        gain_two_grad = jnp.sum(normal_two * middle * scale_two, 0)
        gradient = gradient + norm_back(normal_two, middle, scale_two, gain_two)
        attn_low = gradient.astype(bf16)
        attended_grad = dot_nt(attn_low, w_out).astype(bf16)
        if layer:
            attended_grad = fence(attended_grad, ffn_jobs[1], back)
        else:
            attended_grad = fence(attended_grad, ffn_jobs[0], attn_jobs[1])
        query_grad, kv_grad = attention_backward(
            qk, kv_all, attended_grad, lse, key_info, query_info
        )
        if layer:
            query_grad, kv_grad = fence((query_grad, kv_grad), back)
            kv_grad = scatter_group(kv_grad).reshape(rows, 2 * KV_WIDTH)
            query_grad, kv_grad = fence((query_grad, kv_grad), ffn_jobs[1])
        else:
            query_grad, kv_grad = fence((query_grad, kv_grad), ffn_jobs[0])
            kv_grad = scatter_group(kv_grad).reshape(rows, 2 * KV_WIDTH)
            query_grad, kv_grad = fence((query_grad, kv_grad), attn_jobs[1])
        dw_qk, dw_ov, gain_one_grad, gradient = qkv_backward(
            query_grad, kv_grad, residual, normed_one, scale_one, gain_one, w_qk, w_v,
            cosine, sine, gradient, attended, attn_low,
        )
        if layer:
            dw_qk, dw_ov, gradient = fence((dw_qk, dw_ov, gradient), ffn_jobs[1])
        else:
            dw_qk, dw_ov, gradient = fence((dw_qk, dw_ov, gradient))
        attn_jobs[layer] = Job(
            scatter_attention_job(
                dw_qk, dw_ov, jnp.concatenate([gain_one_grad[0], gain_two_grad]), qkv_len, out_len
            )
        )
    last = Job(pair_tokens_job(gradient.reshape(2, local_len, D), bf16))
    fence((), last)
    fence((), ffn_jobs[0], attn_jobs[0], attn_jobs[1])
    fence((), attn_jobs[0], last)
    fence((), attn_jobs[0], ffn_jobs[0])
    finish((), back, last, *ffn_jobs, *attn_jobs)
    return (
        back.result,
        last.result,
        jnp.stack([job.result[0] for job in attn_jobs]),
        jnp.stack([job.result[1] for job in attn_jobs]),
        jnp.stack([job.result for job in ffn_jobs]),
        jnp.stack([job.result[2] for job in attn_jobs]),
    )


def solution(mesh):
    tokens = P("dp", "ctx", None)
    shards = P(None, ("dp", "ctx"))
    return jax.shard_map(
        per_device,
        mesh=mesh,
        in_specs=(tokens, P("dp", "ctx"), P("dp", "ctx"), shards, shards, shards, shards, tokens),
        out_specs=(tokens, tokens, shards, shards, shards, shards),
        check_vma=False,
    )
```
